128 devices in a mesh: row: 8 (over x, core), col: 16 (over z, y).
Axes of the slice: x: 4, y: 4, z: 4, core: 2. Of those that a mesh axis runs over, the one named last changes fastest.
Arguments:
- tiles: bfloat16 [8, 16, 384, 128, 128], P('row', 'col'), may hold values from -0.15625 to 0.15625
- tile_row: int32 [8, 16, 384], P('row', 'col'), may hold values from 0 to 511, as said below
- tile_col: int32 [8, 16, 384], P('row', 'col'), may hold values from 0 to 255
- tile_count: int32 [8, 16], P('row', 'col'), may hold values from 96 to 384, as said below
- vectors: bfloat16 [32, 8, 16, 4096], P(None, 'row', 'col'), may hold values from -6 to 6
Outputs:
- image: bfloat16 [32, 524288], P(None, ('row', 'col'))
- back_image: bfloat16 [32, 8, 16, 4096], P(None, 'row', 'col')
The draws below stay inside these ranges and needn't reach their ends.
Inputs may be any that keep to these rules, and one draw needn't show every extreme that they name: `tile_count`: some device has exactly 384 live slots. `tile_row`: the slots of each device, live or not, name exactly 12 distinct block rows in each aligned run of 32 block rows.
All inputs are finite; a program needn't handle non-finite values.
Results may differ from the reference program's by a relative error of at most 0.0041.
Values may be sent and summed in bfloat16 or wider, within the bound.
No kernel may reach another device: no remote copies, remote signals or barrier semaphores. Data moves between devices by JAX's collectives and lax.ppermute only.
A program may use at most 128 MiB of HBM per device.

```python
import jax
import jax.numpy as jnp
from jax import lax

TILE = 128
K = 32
BLK_ROWS = 512
TILES_DEV = 384
BLK_COLS = 256
VC = 4096
SHARE = 32
CAP = 12
N_ROW = 8
N_COL = 16


def draw_tile_count(key, part):
    base = jax.random.randint(jax.random.fold_in(key, 11), (N_ROW, N_COL), TILES_DEV // 4, TILES_DEV + 1, dtype=jnp.int32)
    chosen = jax.random.randint(jax.random.fold_in(key, 12), (), 0, N_ROW * N_COL, dtype=jnp.int32)
    places = jnp.arange(N_ROW * N_COL, dtype=jnp.int32).reshape(N_ROW, N_COL)
    return jnp.where(places == chosen, TILES_DEV, base).astype(jnp.int32)


def distinct_order(key, shape):
    length = shape[-1]
    scores = jax.random.randint(key, shape, 0, 1 << 20, dtype=jnp.int32) * length + jnp.arange(length, dtype=jnp.int32)
    return jnp.argsort(scores, axis=-1, stable=True).astype(jnp.int32)


def draw_tile_row(key, part):
    picks = distinct_order(jax.random.fold_in(key, 21), (N_ROW, N_COL, N_COL, SHARE))[..., :CAP]
    owners = jnp.arange(N_COL, dtype=jnp.int32)[None, None, :, None] * SHARE
    chosen = (owners + picks).reshape(N_ROW, N_COL, N_COL * CAP)
    width = N_COL * CAP
    first = jnp.take_along_axis(chosen, distinct_order(jax.random.fold_in(key, 22), (N_ROW, N_COL, width)), axis=-1)
    extra = TILES_DEV - width
    first_draw = jax.random.randint(jax.random.fold_in(key, 23), (N_ROW, N_COL, extra), 0, width, dtype=jnp.int32)
    second_draw = jax.random.randint(jax.random.fold_in(key, 24), (N_ROW, N_COL, extra), 0, width, dtype=jnp.int32)
    skewed = first_draw * second_draw // width
    rest = jnp.take_along_axis(chosen, skewed, axis=-1)
    slots = jnp.concatenate([first, rest], axis=-1)
    order = distinct_order(jax.random.fold_in(key, 25), (N_ROW, N_COL, TILES_DEV))
    return jnp.take_along_axis(slots, order, axis=-1).astype(jnp.int32)


def with_ends(result, stream_key, smallest, high):
    longest = result.shape.index(max(result.shape))
    spots = []
    for shift in (0, 1):
        where = [jax.random.randint(jax.random.fold_in(stream_key, axis), (), 0, length) for axis, length in enumerate(result.shape)]
        where[longest] = (where[longest] + shift) % result.shape[longest]
        spots.append(tuple(where))
    return result.at[spots[0]].set(smallest).at[spots[1]].set(high)


def levels(stream_key, dims, cuts, least, largest):
    loudness, own = 1.0, jax.random.fold_in(stream_key, 6)
    for position, parts in cuts:
        draws = jnp.exp(jax.random.uniform(jax.random.fold_in(own, position), (parts,), jnp.float32, least / len(cuts), largest / len(cuts)))
        loudness = loudness * jnp.repeat(draws, dims[position] // parts).reshape([-1 if axis == position else 1 for axis in range(len(dims))])
    return loudness


def scatter_about(key, shape, spread, reach, shards=(), held_as=jnp.bfloat16):
    gain = levels(key, shape, shards, -0.22, 0.18) if shards else 1.0
    values = jax.random.normal(key, shape, jnp.float32) * spread * gain
    return jnp.minimum(jnp.maximum(values, -reach), reach).astype(held_as)


def setup_inputs(seed: int = 0) -> dict:
    key_list = jax.random.split(jax.random.key(seed), 6)
    tiles = scatter_about(key_list[0], (N_ROW, N_COL, TILES_DEV, TILE, TILE), (TILE * max(1, TILES_DEV * N_COL // BLK_ROWS)) ** -0.5, 0.15625, ((0, 8), (1, 16)))
    tile_row = draw_tile_row(jax.random.fold_in(key_list[5], 71), 0)
    tile_col = with_ends(jax.random.randint(key_list[2], (N_ROW, N_COL, TILES_DEV), 0, BLK_COLS), jax.random.fold_in(key_list[2], 1), 0, BLK_COLS - 1).astype(jnp.int32)
    tile_count = draw_tile_count(jax.random.fold_in(key_list[5], 71), 0)
    vectors = scatter_about(key_list[4], (K, N_ROW, N_COL, VC), 1.0, 6.0, ((1, 8), (2, 16)))
    return dict(tiles=tiles, tile_row=tile_row, tile_col=tile_col, tile_count=tile_count, vectors=vectors)


def reference(tiles, tile_row, tile_col, tile_count, vectors):
    block_total = BLK_ROWS * N_ROW
    row_ids = jnp.arange(N_ROW, dtype=jnp.int32)[:, None, None]
    col_ids = jnp.arange(N_COL, dtype=jnp.int32)[None, :, None]
    slot_ids = jnp.arange(TILES_DEV, dtype=jnp.int32)[None, None, :]
    global_rows = (row_ids * BLK_ROWS + tile_row).reshape(-1).astype(jnp.int32)
    global_cols = (col_ids * BLK_COLS + tile_col).reshape(-1).astype(jnp.int32)
    live_mask = (slot_ids < tile_count[:, :, None]).astype(jnp.float32).reshape(-1)
    flat_tiles = tiles.reshape(-1, TILE, TILE)
    slot_total = flat_tiles.shape[0]
    group_size = 64 if slot_total % 64 == 0 else TILES_DEV
    group_count = slot_total // group_size
    vec_blocks = vectors.astype(jnp.float32).transpose(0, 2, 1, 3).reshape(K, block_total, TILE).transpose(1, 0, 2)

    def pieces(turn):
        start = (turn * group_size).astype(jnp.int32)
        tile_block = lax.dynamic_slice_in_dim(flat_tiles, start, group_size, 0).astype(jnp.float32)
        rows_here = lax.dynamic_slice_in_dim(global_rows, start, group_size, 0)
        cols_here = lax.dynamic_slice_in_dim(global_cols, start, group_size, 0)
        mask_here = lax.dynamic_slice_in_dim(live_mask, start, group_size, 0)
        return tile_block, rows_here, cols_here, mask_here

    def forward(totals, turn):
        tile_block, rows_here, cols_here, mask_here = pieces(turn)
        picked = vec_blocks[cols_here]
        product = jnp.einsum('skj,sij->ski', picked, tile_block) * mask_here[:, None, None]
        return totals.at[rows_here].add(product), None

    turns = jnp.arange(group_count, dtype=jnp.int32)
    forward_sum, _ = lax.scan(forward, jnp.zeros((block_total, K, TILE), jnp.float32), turns)
    image_blocks = forward_sum.astype(jnp.bfloat16)
    image_wide = image_blocks.astype(jnp.float32)

    def backward(totals, turn):
        tile_block, rows_here, cols_here, mask_here = pieces(turn)
        picked = image_wide[rows_here]
        product = jnp.einsum('ski,sij->skj', picked, tile_block) * mask_here[:, None, None]
        return totals.at[cols_here].add(product), None

    backward_sum, _ = lax.scan(backward, jnp.zeros((block_total, K, TILE), jnp.float32), turns)
    image = image_blocks.transpose(1, 0, 2).reshape(K, block_total * TILE)
    back_image = backward_sum.astype(jnp.bfloat16).transpose(1, 0, 2).reshape(K, N_COL, N_ROW, VC).transpose(0, 2, 1, 3)
    return image, back_image
```

```python
import jax
import jax.numpy as jnp
from jax import lax
from jax.experimental import pallas as pl
from jax.experimental.pallas import tpu as pltpu
from jax.sharding import PartitionSpec as P

TILE = 128
K = 32
SHARE = 32
CAP = 12
N_COL = 16
N_X = 4
RUN_ROWS = CAP * K
PAY_ROWS = RUN_ROWS + 16
N_NAMED = N_COL * CAP
GROUP = 8
CHUNK = 32
VMEM_LIMIT = 56 << 20


def tile_copy(tiles, buf, sems, chunk):
    span = pl.ds(chunk * CHUNK, CHUNK)
    return pltpu.make_async_copy(tiles.at[span], buf.at[span], sems.at[chunk])


def start_tiles(tiles, buf, sems, live):
    for chunk in range(tiles.shape[0] // CHUNK):
        @pl.when(chunk * CHUNK < live)
        def _():
            tile_copy(tiles, buf, sems, chunk).start()


def sweep(live, tiles, buf, sems, left, left_index, total, total_index, dims):
    def group(g, _):
        @pl.when(g % (CHUNK // GROUP) == 0)
        def _():
            tile_copy(tiles, buf, sems, g // (CHUNK // GROUP)).wait()

        base = g * GROUP
        products = [
            lax.dot_general(
                left[left_index[base + u]],
                buf[base + u],
                (((1,), (dims,)), ((), ())),
                preferred_element_type=jnp.float32,
            )
            for u in range(GROUP)
        ]
        for u in range(GROUP):
            total[total_index[base + u]] += products[u]
        return 0

    lax.fori_loop(0, (live + GROUP - 1) // GROUP, group, 0)


def forward_kernel(rowc, cols, scal, tiles, ids, *refs):
    pieces, (send, vec, total, buf, sems) = refs[:8], refs[8:]
    live, x, core = scal[0], scal[1], scal[2]
    start_tiles(tiles, buf, sems, live)
    for d in range(N_X):
        for other in range(2):
            piece = pieces[d + N_X * other]
            first = (((x + d) % N_X) * 2 + (core + other) % 2) * SHARE
            for b in range(SHARE):
                vec[first + b] = piece[:, b * TILE:(b + 1) * TILE]

    def clear(p, _):
        total[p] = jnp.zeros((K, TILE), jnp.float32)
        return 0

    lax.fori_loop(0, N_NAMED, clear, 0, unroll=8)
    sweep(live, tiles, buf, sems, vec, cols, total, rowc, 1)

    def pack(c, _):
        for q in range(CAP):
            send[c, q * K:(q + 1) * K] = total[c * CAP + q].astype(jnp.bfloat16)
        send[c, RUN_ROWS:] = ids[c]
        return 0

    lax.fori_loop(0, N_COL, pack, 0)


def reduce_kernel(recv, image, send, total, blocks, wide_ids, ids, sem):
    for c in range(N_COL):
        wide_ids[c:c + 1] = recv[c, RUN_ROWS:][0:1].astype(jnp.float32).astype(jnp.int32)
    copy = pltpu.make_async_copy(wide_ids, ids, sem)
    copy.start()
    for b in range(SHARE):
        total[b] = jnp.zeros((K, TILE), jnp.float32)
    copy.wait()

    def add(c, _):
        for q in range(CAP):
            total[ids[c, q]] += recv[c, q * K:(q + 1) * K].astype(jnp.float32)
        return 0

    lax.fori_loop(0, N_COL, add, 0)
    for b in range(SHARE):
        block = total[b].astype(jnp.bfloat16)
        blocks[b] = block
        image[:, b * TILE:(b + 1) * TILE] = block

    def spread(c, _):
        for q in range(CAP):
            send[c, q * K:(q + 1) * K] = blocks[ids[c, q]]
        return 0

    lax.fori_loop(0, N_COL, spread, 0)


def backward_kernel(rowc, colx, scal, tiles, recv, keep, give, total, buf, sems):
    live, core = scal[0], scal[2]
    start_tiles(tiles, buf, sems, live)

    def clear(p, _):
        total[p] = jnp.zeros((K, TILE), jnp.float32)
        return 0

    lax.fori_loop(0, 2 * N_X * SHARE, clear, 0, unroll=8)
    sweep(live, tiles, buf, sems, recv, rowc, total, colx, 0)

    def split(b, _):
        for x in range(N_X):
            keep[x, b] = total[(x * 2 + core) * SHARE + b]
            give[x, b] = total[(x * 2 + 1 - core) * SHARE + b].astype(give.dtype)
        return 0

    lax.fori_loop(0, SHARE, split, 0, unroll=4)


def pair_kernel(scal, keep, got, own, one, two, three):
    x = scal[1]

    def step(b, _):
        for d, out in enumerate((own, one, two, three)):
            to = (x + d) % N_X
            out[b] = (keep[to, b] + got[to, b].astype(jnp.float32)).astype(out.dtype)
        return 0

    lax.fori_loop(0, SHARE, step, 0, unroll=2)


def final_kernel(own, one, two, three, out):
    for b in range(SHARE):
        total = own[b] + one[b].astype(jnp.float32)
        total = total + two[b].astype(jnp.float32) + three[b].astype(jnp.float32)
        out[:, b * TILE:(b + 1) * TILE] = total.astype(jnp.bfloat16)


def call(kernel, outs, scalars, arrays, scratch=(), tiles=False):
    spec_any = pl.BlockSpec(memory_space=pl.ANY)
    spec_vmem = pl.BlockSpec(memory_space=pltpu.VMEM)
    spec_smem = pl.BlockSpec(memory_space=pltpu.SMEM)
    specs = [spec_smem] * len(scalars)
    specs += [spec_any if tiles and i == 0 else spec_vmem for i in range(len(arrays))]
    single = not isinstance(outs, (list, tuple))
    return pl.pallas_call(
        kernel,
        out_shape=outs,
        in_specs=specs,
        out_specs=spec_vmem if single else [spec_vmem] * len(outs),
        scratch_shapes=list(scratch),
        compiler_params=pltpu.CompilerParams(vmem_limit_bytes=VMEM_LIMIT),
    )(*scalars, *arrays)


def named_rows(rows):
    hits = rows[:, None] == jnp.arange(N_COL * SHARE, dtype=jnp.int32)[None, :]
    present = jnp.any(hits, axis=0).astype(jnp.int32).reshape(N_COL, SHARE)
    place = jnp.arange(SHARE, dtype=jnp.int32)
    rank = jnp.sum(jnp.where(place[:, None] < place[None, :], present[:, :, None], 0), axis=1)
    match = (rank[:, None, :] == jnp.arange(CAP, dtype=jnp.int32)[None, :, None]) & (present[:, None, :] > 0)
    ids = jnp.sum(jnp.where(match, place[None, None, :], 0), axis=2)
    position = (rank + CAP * jnp.arange(N_COL, dtype=jnp.int32)[:, None]).reshape(-1)
    rowc = jnp.sum(jnp.where(hits, position[None, :], 0), axis=1)
    return ids, rowc


def per_device(tiles, tile_row, tile_col, tile_count, vectors):
    bf16, f32 = jnp.bfloat16, jnp.float32
    shape = jax.ShapeDtypeStruct
    local = tiles[0, 0]
    slots = local.shape[0]
    rows, cols, live = tile_row[0, 0], tile_col[0, 0], tile_count[0, 0]
    row_at = lax.axis_index("row")
    scal = jnp.stack([live, row_at // 2, row_at % 2]).astype(jnp.int32)

    def along_x(value, d):
        return lax.ppermute(value, "row", [(i, (i - 2 * d) % 8) for i in range(8)])

    def swap_core(value):
        return lax.ppermute(value, "row", [(i, i ^ 1) for i in range(8)])

    mine = vectors.reshape(K, SHARE * TILE)
    near = [mine] + [along_x(mine, d) for d in range(1, N_X)]
    pieces = near + [swap_core(v) for v in near]

    ids, rowc = named_rows(rows)
    alive = jnp.arange(slots, dtype=jnp.int32) < live
    row_to = jnp.where(alive, rowc, N_NAMED)
    col_to = jnp.where(alive, cols, 2 * N_X * SHARE)
    lanes = jnp.pad(ids, ((0, 0), (0, TILE - CAP))).astype(bf16)
    id_rows = jnp.broadcast_to(lanes[:, None, :], (N_COL, 16, TILE))

    tile_scratch = [pltpu.VMEM((slots, TILE, TILE), bf16), pltpu.SemaphoreType.DMA((slots // CHUNK,))]
    send = call(
        forward_kernel,
        shape((N_COL, PAY_ROWS, TILE), bf16),
        [row_to, cols, scal],
        [local, id_rows] + pieces,
        [pltpu.VMEM((2 * N_X * SHARE, K, TILE), bf16), pltpu.VMEM((N_NAMED + 1, K, TILE), f32)] + tile_scratch,
        tiles=True,
    )
    recv = lax.all_to_all(send, "col", 0, 0, tiled=True)
    image, spread = call(
        reduce_kernel,
        [shape((K, SHARE * TILE), bf16), shape((N_COL, RUN_ROWS, TILE), bf16)],
        [],
        [recv],
        [
            pltpu.VMEM((SHARE, K, TILE), f32),
            pltpu.VMEM((SHARE, K, TILE), bf16),
            pltpu.VMEM((N_COL, TILE), jnp.int32),
            pltpu.SMEM((N_COL, TILE), jnp.int32),
            pltpu.SemaphoreType.DMA,
        ],
    )
    named = lax.all_to_all(spread, "col", 0, 0, tiled=True).reshape(N_NAMED, K, TILE)
    keep, give = call(
        backward_kernel,
        [shape((N_X, SHARE, K, TILE), f32), shape((N_X, SHARE, K, TILE), bf16)],
        [rowc, col_to, scal],
        [local, named],
        [pltpu.VMEM((2 * N_X * SHARE + 1, K, TILE), f32)] + tile_scratch,
        tiles=True,
    )
    got = swap_core(give)
    block = (SHARE, K, TILE)
    own, *away = call(
        pair_kernel, [shape(block, f32)] + [shape(block, bf16)] * 3, [scal], [keep, got]
    )
    parts = [lax.ppermute(v, "row", [(i, (i + 2 * d) % 8) for i in range(8)]) for d, v in enumerate(away, 1)]
    back = call(final_kernel, shape((K, SHARE * TILE), bf16), [], [own] + parts)
    return image, back.reshape(vectors.shape)


def solution(mesh):
    return jax.shard_map(
        per_device,
        mesh=mesh,
        in_specs=(
            P("row", "col", None, None, None),
            P("row", "col", None),
            P("row", "col", None),
            P("row", "col"),
            P(None, "row", "col", None),
        ),
        out_specs=(P(None, ("row", "col")), P(None, "row", "col", None)),
        check_vma=False,
    )
```

```python
import jax
import jax.numpy as jnp
from jax import lax
from jax.experimental import pallas as pl
from jax.experimental.pallas import tpu as pltpu
from jax.sharding import PartitionSpec as P

TILE = 128
K = 32
SHARE = 32
CAP = 12
N_COL = 16
N_X = 4
RUN_ROWS = CAP * K
PAY_ROWS = RUN_ROWS + 16
N_NAMED = N_COL * CAP
GROUP = 32
CHUNK = 32
NEAR = (0, 1, 3)


def fetch_kernel(scal, tiles, out, sems):
    live = scal[0]

    def copy(chunk):
        span = pl.ds(chunk * CHUNK, CHUNK)
        return pltpu.make_async_copy(tiles.at[span], out.at[span], sems.at[chunk])

    chunks = range(tiles.shape[0] // CHUNK)
    for chunk in chunks:
        @pl.when(chunk * CHUNK < live)
        def _():
            copy(chunk).start()
    for chunk in chunks:
        @pl.when(chunk * CHUNK < live)
        def _():
            copy(chunk).wait()


def code_parts(code):
    return code & 511, (code >> 9) & 255, (code >> 17) & 255, code >> 25


def sweep(count, codes, tiles, left, total, spots, dims):
    def group(g, _):
        base = g * GROUP
        products, places = [], []
        for u in range(GROUP):
            slot, source, place = spots(*code_parts(codes[base + u]))
            places.append(place)
            products.append(
                lax.dot_general(
                    left[source],
                    tiles[slot],
                    (((1,), (dims,)), ((), ())),
                    preferred_element_type=jnp.float32,
                )
            )
        for place, product in zip(places, products):
            total[place] += product
        return 0

    lax.fori_loop(0, (count + GROUP - 1) // GROUP, group, 0)


def clear_blocks(total, count):
    def clear(p, _):
        total[p] = jnp.zeros((K, TILE), jnp.float32)
        return 0

    lax.fori_loop(0, count, clear, 0, unroll=8)


def forward_spots(blocks):
    return lambda slot, row, col, spare: (slot, col & (blocks - 1), row + N_NAMED * spare)


def forward_near_kernel(codes, scal, tiles, *refs):
    pieces, (total, vec) = refs[:6], refs[6:]
    x, core = scal[1], scal[2]
    for i, d in enumerate(NEAR):
        for other in range(2):
            piece = pieces[i + 3 * other]
            first = (((x + d) % N_X) * 2 + (core + other) % 2) * SHARE
            for b in range(SHARE):
                vec[first + b] = piece[:, b * TILE:(b + 1) * TILE]
    clear_blocks(total, N_NAMED)
    sweep(scal[3], codes, tiles, vec, total, forward_spots(2 * N_X * SHARE), 1)


def forward_far_kernel(codes, scal, tiles, ids, here, there, begun, send, total, vec):
    core = scal[2]
    for other, piece in enumerate((here, there)):
        first = ((core + other) % 2) * SHARE
        for b in range(SHARE):
            vec[first + b] = piece[:, b * TILE:(b + 1) * TILE]
    sweep(scal[4], codes, tiles, vec, total, forward_spots(2 * SHARE), 1)

    def pack(c, _):
        for q in range(CAP):
            send[c, q * K:(q + 1) * K] = total[c * CAP + q].astype(jnp.bfloat16)
        send[c, RUN_ROWS:] = ids[c]
        return 0

    lax.fori_loop(0, N_COL, pack, 0)


def reduce_kernel(recv, image, send, total, blocks, wide_ids, ids, sem):
    for c in range(N_COL):
        wide_ids[c:c + 1] = recv[c, RUN_ROWS:][0:1].astype(jnp.float32).astype(jnp.int32)
    copy = pltpu.make_async_copy(wide_ids, ids, sem)
    copy.start()
    for b in range(SHARE):
        total[b] = jnp.zeros((K, TILE), jnp.float32)
    copy.wait()

    def add(c, _):
        for q in range(CAP):
            total[ids[c, q]] += recv[c, q * K:(q + 1) * K].astype(jnp.float32)
        return 0

    lax.fori_loop(0, N_COL, add, 0)
    for b in range(SHARE):
        block = total[b].astype(jnp.bfloat16)
        blocks[b] = block
        image[:, b * TILE:(b + 1) * TILE] = block

    def spread(c, _):
        for q in range(CAP):
            send[c, q * K:(q + 1) * K] = blocks[ids[c, q]]
        return 0

    lax.fori_loop(0, N_COL, spread, 0)


def backward_spots(blocks):
    return lambda slot, row, col, spare: (slot, row, (col & (blocks - 1)) + blocks * spare)


def backward_far_kernel(codes, scal, tiles, recv, keep, give, total):
    core = scal[2]
    clear_blocks(total, 2 * SHARE)
    sweep(scal[4], codes, tiles, recv, total, backward_spots(2 * SHARE), 0)

    def split(b, _):
        keep[b] = total[core * SHARE + b]
        give[b] = total[(1 - core) * SHARE + b].astype(give.dtype)
        return 0

    lax.fori_loop(0, SHARE, split, 0, unroll=4)


def backward_near_kernel(codes, scal, tiles, recv, keep, give, total):
    x, core = scal[1], scal[2]
    clear_blocks(total, 2 * N_X * SHARE)
    sweep(scal[3], codes, tiles, recv, total, backward_spots(2 * N_X * SHARE), 0)

    def split(b, _):
        for i, d in enumerate(NEAR):
            first = ((x + d) % N_X) * 2 * SHARE + b
            keep[i, b] = total[first + core * SHARE]
            give[i, b] = total[first + (1 - core) * SHARE].astype(give.dtype)
        return 0

    lax.fori_loop(0, SHARE, split, 0, unroll=4)


def far_pair_kernel(keep, got, out):
    def step(b, _):
        out[b] = (keep[b] + got[b].astype(jnp.float32)).astype(out.dtype)
        return 0

    lax.fori_loop(0, SHARE, step, 0, unroll=8)


def near_pair_kernel(keep, got, own, one, three):
    def step(b, _):
        for i, out in enumerate((own, one, three)):
            out[b] = (keep[i, b] + got[i, b].astype(jnp.float32)).astype(out.dtype)
        return 0

    lax.fori_loop(0, SHARE, step, 0, unroll=4)


def final_kernel(own, one, two, three, out):
    for b in range(SHARE):
        total = own[b] + one[b].astype(jnp.float32)
        total = total + two[b].astype(jnp.float32) + three[b].astype(jnp.float32)
        out[:, b * TILE:(b + 1) * TILE] = total.astype(jnp.bfloat16)


def call(kernel, outs, scalars, arrays, scratch=(), limit=8, hbm=False, aliases=None):
    spec_vmem = pl.BlockSpec(memory_space=pltpu.VMEM)
    spec_smem = pl.BlockSpec(memory_space=pltpu.SMEM)
    spec_hbm = pl.BlockSpec(memory_space=pltpu.HBM)
    specs = [spec_smem] * len(scalars) + [spec_hbm if hbm else spec_vmem] * len(arrays)
    single = not isinstance(outs, (list, tuple))
    return pl.pallas_call(
        kernel,
        out_shape=outs,
        in_specs=specs,
        out_specs=spec_vmem if single else [spec_vmem] * len(outs),
        scratch_shapes=list(scratch),
        input_output_aliases=aliases or {},
        compiler_params=pltpu.CompilerParams(vmem_limit_bytes=limit << 20),
    )(*scalars, *arrays)


def slot_lists(rowc, cols, live, x):
    slot = jnp.arange(rowc.shape[0], dtype=jnp.int32)
    code = slot | (rowc << 9) | (cols << 17)
    far = (((cols >> 6) - x) & (N_X - 1)) == 2
    member = jnp.stack([(slot < live) & ~far, (slot < live) & far])
    earlier = slot[:, None] < slot[None, :]
    place = jnp.sum(jnp.where(member[:, :, None] & earlier[None], 1, 0), axis=1)
    match = member[:, :, None] & (place[:, :, None] == slot[None, None, :])
    packed = jnp.sum(jnp.where(match, code[None, :, None], 0), axis=1)
    counts = jnp.sum(member.astype(jnp.int32), axis=1)
    return jnp.where(slot[None, :] < counts[:, None], packed, 1 << 25), counts


def named_rows(rows):
    hits = rows[:, None] == jnp.arange(N_COL * SHARE, dtype=jnp.int32)[None, :]
    present = jnp.any(hits, axis=0).astype(jnp.int32).reshape(N_COL, SHARE)
    place = jnp.arange(SHARE, dtype=jnp.int32)
    rank = jnp.sum(jnp.where(place[:, None] < place[None, :], present[:, :, None], 0), axis=1)
    match = (rank[:, None, :] == jnp.arange(CAP, dtype=jnp.int32)[None, :, None]) & (present[:, None, :] > 0)
    ids = jnp.sum(jnp.where(match, place[None, None, :], 0), axis=2)
    position = (rank + CAP * jnp.arange(N_COL, dtype=jnp.int32)[:, None]).reshape(-1)
    rowc = jnp.sum(jnp.where(hits, position[None, :], 0), axis=1)
    return ids, rowc


def per_device(tiles, tile_row, tile_col, tile_count, vectors):
    bf16, f32 = jnp.bfloat16, jnp.float32
    shape = jax.ShapeDtypeStruct
    local = tiles[0, 0]
    rows, cols, live = tile_row[0, 0], tile_col[0, 0], tile_count[0, 0]
    row_at = lax.axis_index("row")
    x, core = row_at // 2, row_at % 2

    def along_x(value, d):
        return lax.ppermute(value, "row", [(i, (i + 2 * d) % 8) for i in range(8)])

    def swap_core(value):
        return lax.ppermute(value, "row", [(i, i ^ 1) for i in range(8)])

    mine = vectors.reshape(K, SHARE * TILE)
    near = [mine, along_x(mine, -1), along_x(mine, 1)]
    far = along_x(mine, 2)
    first = jnp.stack([live]).astype(jnp.int32)
    held = call(
        fetch_kernel, shape(local.shape, bf16), [first],
        [pltpu.with_memory_space_constraint(local, pltpu.HBM)],
        [pltpu.SemaphoreType.DMA((local.shape[0] // CHUNK,))], limit=1, hbm=True,
    )

    ids, rowc = named_rows(rows)
    codes, counts = slot_lists(rowc, cols, live, x)
    scal = jnp.stack([live, x, core, counts[0], counts[1]]).astype(jnp.int32)
    near_codes, far_codes = codes[0], codes[1]
    lanes = jnp.pad(ids, ((0, 0), (0, TILE - CAP))).astype(bf16)
    id_rows = jnp.broadcast_to(lanes[:, None, :], (N_COL, 16, TILE))
    near, near_codes, far_codes, id_rows, scal, held = lax.optimization_barrier(
        (near, near_codes, far_codes, id_rows, scal, held)
    )

    begun = call(
        forward_near_kernel,
        shape((N_NAMED + 1, K, TILE), f32),
        [near_codes, scal],
        [held] + near + [swap_core(v) for v in near],
        [pltpu.VMEM((2 * N_X * SHARE, K, TILE), bf16)],
    )
    far, begun = lax.optimization_barrier((far, begun))
    send, _ = call(
        forward_far_kernel,
        [shape((N_COL, PAY_ROWS, TILE), bf16), shape((N_NAMED + 1, K, TILE), f32)],
        [far_codes, scal],
        [held, id_rows, far, swap_core(far), begun],
        [pltpu.VMEM((2 * SHARE, K, TILE), bf16)],
        aliases={6: 1},
    )
    recv = lax.all_to_all(send, "col", 0, 0, tiled=True)
    image, spread = call(
        reduce_kernel,
        [shape((K, SHARE * TILE), bf16), shape((N_COL, RUN_ROWS, TILE), bf16)],
        [],
        [recv],
        [
            pltpu.VMEM((SHARE, K, TILE), f32),
            pltpu.VMEM((SHARE, K, TILE), bf16),
            pltpu.VMEM((N_COL, TILE), jnp.int32),
            pltpu.SMEM((N_COL, TILE), jnp.int32),
            pltpu.SemaphoreType.DMA,
        ],
    )
    named = lax.all_to_all(spread, "col", 0, 0, tiled=True).reshape(N_NAMED, K, TILE)

    block = (SHARE, K, TILE)
    keep, give = call(
        backward_far_kernel,
        [shape(block, f32), shape(block, bf16)],
        [far_codes, scal],
        [held, named],
        [pltpu.VMEM((2 * SHARE + 1, K, TILE), f32)],
    )
    away = call(far_pair_kernel, shape(block, bf16), [], [keep, swap_core(give)])
    away, named = lax.optimization_barrier((away, named))
    two = along_x(away, 2)
    keep, give = call(
        backward_near_kernel,
        [shape((3,) + block, f32), shape((3,) + block, bf16)],
        [near_codes, scal],
        [held, named],
        [pltpu.VMEM((2 * N_X * SHARE + 1, K, TILE), f32)],
    )
    own, one, three = call(
        near_pair_kernel,
        [shape(block, f32), shape(block, bf16), shape(block, bf16)],
        [],
        [keep, swap_core(give)],
    )
    one, three = along_x(one, 1), along_x(three, -1)
    back = call(final_kernel, shape((K, SHARE * TILE), bf16), [], [own, one, two, three])
    return image, back.reshape(vectors.shape)


def solution(mesh):
    return jax.shard_map(
        per_device,
        mesh=mesh,
        in_specs=(
            P("row", "col", None, None, None),
            P("row", "col", None),
            P("row", "col", None),
            P("row", "col"),
            P(None, "row", "col", None),
        ),
        out_specs=(P(None, ("row", "col")), P(None, "row", "col", None)),
        check_vma=False,
    )
```

```python
import jax
import jax.numpy as jnp
from jax import lax
from jax.experimental import pallas as pl
from jax.experimental.pallas import tpu as pltpu
from jax.sharding import PartitionSpec as P

TILE = 128
K = 32
SHARE = 32
CAP = 12
N_COL = 16
N_X = 4
RUN_ROWS = CAP * K
PAY_ROWS = RUN_ROWS + 16
N_NAMED = N_COL * CAP
GROUP = 32
CHUNK = 32
NEAR = (0, 1, 3)
PARTS = 2
LONG = pl.CostEstimate(flops=1 << 36, transcendentals=0, bytes_accessed=1 << 26)


def tile_copy(tiles, held, sems, chunk):
    span = pl.ds(pl.multiple_of(chunk * CHUNK, CHUNK), CHUNK)
    return pltpu.make_async_copy(tiles.at[span], held.at[span], sems.at[chunk])


def code_parts(code):
    return code & 511, (code >> 9) & 255, (code >> 17) & 255, code >> 25


def sweep(count, codes, tiles, left, total, spots, dims, ready=None):
    def group(g, seen):
        base = g * GROUP
        if ready is not None:
            seen = ready(seen, (codes[jnp.minimum(base + GROUP, count) - 1] & 511) // CHUNK + 1)
        products, places = [], []
        for u in range(GROUP):
            slot, source, place = spots(*code_parts(codes[base + u]))
            places.append(place)
            products.append(
                lax.dot_general(
                    left[source],
                    tiles[slot],
                    (((1,), (dims,)), ((), ())),
                    preferred_element_type=jnp.float32,
                )
            )
        for place, product in zip(places, products):
            total[place] += product
        return seen

    return lax.fori_loop(0, (count + GROUP - 1) // GROUP, group, 0)


def clear_blocks(total, count):
    def clear(p, _):
        total[p] = jnp.zeros((K, TILE), jnp.float32)
        return 0

    lax.fori_loop(0, count, clear, 0, unroll=8)


def forward_spots(blocks):
    return lambda slot, row, col, spare: (slot, col & (blocks - 1), row + N_NAMED * spare)


def forward_near_kernel(codes, scal, tiles, *refs):
    pieces, (total, held, vec, sems) = refs[:6], refs[6:]
    live, x, core = scal[0], scal[1], scal[2]
    chunks = (live + CHUNK - 1) // CHUNK

    def start(chunk, _):
        tile_copy(tiles, held, sems, chunk).start()
        return 0

    def wait(chunk, _):
        tile_copy(tiles, held, sems, chunk).wait()
        return 0

    def ready(seen, need):
        lax.fori_loop(seen, need, wait, 0)
        return jnp.maximum(seen, need)

    lax.fori_loop(0, chunks, start, 0)
    for i, d in enumerate(NEAR):
        for other in range(2):
            piece = pieces[i + 3 * other]
            first = (((x + d) % N_X) * 2 + (core + other) % 2) * SHARE
            for b in range(SHARE):
                vec[first + b] = piece[:, b * TILE:(b + 1) * TILE]
    clear_blocks(total, N_NAMED)
    seen = sweep(scal[3], codes, held, vec, total, forward_spots(2 * N_X * SHARE), 1, ready)
    lax.fori_loop(seen, chunks, wait, 0)


def forward_far_kernel(codes, scal, tiles, ids, here, there, begun, send, total, vec):
    core = scal[2]
    for other, piece in enumerate((here, there)):
        first = ((core + other) % 2) * SHARE
        for b in range(SHARE):
            vec[first + b] = piece[:, b * TILE:(b + 1) * TILE]
    sweep(scal[4], codes, tiles, vec, total, forward_spots(2 * SHARE), 1)

    def pack(c, _):
        for q in range(CAP):
            send[c, q * K:(q + 1) * K] = total[c * CAP + q].astype(jnp.bfloat16)
        send[c, RUN_ROWS:] = ids[c]
        return 0

    lax.fori_loop(0, N_COL, pack, 0)


def reduce_kernel(recv, image, send, total, blocks, wide_ids, ids, sem):
    for c in range(N_COL):
        wide_ids[c:c + 1] = recv[c, RUN_ROWS:][0:1].astype(jnp.float32).astype(jnp.int32)
    copy = pltpu.make_async_copy(wide_ids, ids, sem)
    copy.start()
    for b in range(SHARE):
        total[b] = jnp.zeros((K, TILE), jnp.float32)
    copy.wait()

    def add(c, _):
        for q in range(CAP):
            total[ids[c, q]] += recv[c, q * K:(q + 1) * K].astype(jnp.float32)
        return 0

    lax.fori_loop(0, N_COL, add, 0)
    for b in range(SHARE):
        block = total[b].astype(jnp.bfloat16)
        blocks[b] = block
        image[:, b * TILE:(b + 1) * TILE] = block

    def spread(c, _):
        for q in range(CAP):
            send[c, q * K:(q + 1) * K] = blocks[ids[c, q]]
        return 0

    lax.fori_loop(0, N_COL, spread, 0)


def backward_spots(blocks):
    return lambda slot, row, col, spare: (slot, row, (col & (blocks - 1)) + blocks * spare)


def backward_near_kernel(codes, scal, tiles, recv, keep, give, total):
    x, core = scal[1], scal[2]
    for d in NEAR:
        clear_blocks(total.at[pl.ds(((x + d) % N_X) * 2 * SHARE, 2 * SHARE)], 2 * SHARE)
    sweep(scal[3], codes, tiles, recv, total, backward_spots(2 * N_X * SHARE), 0)

    def split(b, _):
        for i, d in enumerate(NEAR):
            first = ((x + d) % N_X) * 2 * SHARE + b
            keep[i, b] = total[first + core * SHARE]
            give[i, b] = total[first + (1 - core) * SHARE].astype(give.dtype)
        return 0

    lax.fori_loop(0, SHARE, split, 0, unroll=4)


def backward_far_kernel(codes, scal, tiles, recv, keep, *rest):
    gives, total = rest[:-1], rest[-1]
    core = scal[2]
    clear_blocks(total, 2 * SHARE)
    sweep(scal[4], codes, tiles, recv, total, backward_spots(2 * SHARE), 0)
    part = SHARE // len(gives)

    def split(b, _):
        for i, give in enumerate(gives):
            keep[i * part + b] = total[core * SHARE + i * part + b]
            give[b] = total[(1 - core) * SHARE + i * part + b].astype(give.dtype)
        return 0

    lax.fori_loop(0, part, split, 0, unroll=2)


def near_pair_kernel(keep, got, own, one, three):
    def step(b, _):
        for i, out in enumerate((own, one, three)):
            out[b] = (keep[i, b] + got[i, b].astype(jnp.float32)).astype(out.dtype)
        return 0

    lax.fori_loop(0, SHARE, step, 0, unroll=4)


def far_pair_kernel(keep, *rest):
    gots, out = rest[:-1], rest[-1]
    part = SHARE // len(gots)

    def step(b, _):
        for i, got in enumerate(gots):
            out[i * part + b] = (keep[i * part + b] + got[b].astype(jnp.float32)).astype(out.dtype)
        return 0

    lax.fori_loop(0, part, step, 0, unroll=2)


def near_sum_kernel(own, one, three, out):
    def step(b, _):
        out[b] = own[b] + one[b].astype(jnp.float32) + three[b].astype(jnp.float32)
        return 0

    lax.fori_loop(0, SHARE, step, 0, unroll=4)


def final_kernel(begun, two, out):
    for b in range(SHARE):
        total = begun[b] + two[b].astype(jnp.float32)
        out[:, b * TILE:(b + 1) * TILE] = total.astype(jnp.bfloat16)


def call(kernel, outs, scalars, arrays, scratch=(), limit=8, hbm=(), aliases=None, cost=None):
    spec_vmem = pl.BlockSpec(memory_space=pltpu.VMEM)
    spec_smem = pl.BlockSpec(memory_space=pltpu.SMEM)
    spec_hbm = pl.BlockSpec(memory_space=pltpu.HBM)
    specs = [spec_smem] * len(scalars)
    specs += [spec_hbm if i in hbm else spec_vmem for i in range(len(arrays))]
    single = not isinstance(outs, (list, tuple))
    return pl.pallas_call(
        kernel,
        out_shape=outs,
        in_specs=specs,
        out_specs=spec_vmem if single else [spec_vmem] * len(outs),
        scratch_shapes=list(scratch),
        input_output_aliases=aliases or {},
        cost_estimate=cost,
        compiler_params=pltpu.CompilerParams(vmem_limit_bytes=limit << 20),
    )(*scalars, *arrays)


def slot_lists(rowc, cols, live, x):
    slot = jnp.arange(rowc.shape[0], dtype=jnp.int32)
    code = slot | (rowc << 9) | (cols << 17)
    far = (((cols >> 6) - x) & (N_X - 1)) == 2
    member = jnp.stack([(slot < live) & ~far, (slot < live) & far])
    earlier = slot[:, None] < slot[None, :]
    place = jnp.sum(jnp.where(member[:, :, None] & earlier[None], 1, 0), axis=1)
    match = member[:, :, None] & (place[:, :, None] == slot[None, None, :])
    packed = jnp.sum(jnp.where(match, code[None, :, None], 0), axis=1)
    counts = jnp.sum(member.astype(jnp.int32), axis=1)
    return jnp.where(slot[None, :] < counts[:, None], packed, 1 << 25), counts


def named_rows(rows):
    hits = rows[:, None] == jnp.arange(N_COL * SHARE, dtype=jnp.int32)[None, :]
    present = jnp.any(hits, axis=0).astype(jnp.int32).reshape(N_COL, SHARE)
    place = jnp.arange(SHARE, dtype=jnp.int32)
    rank = jnp.sum(jnp.where(place[:, None] < place[None, :], present[:, :, None], 0), axis=1)
    match = (rank[:, None, :] == jnp.arange(CAP, dtype=jnp.int32)[None, :, None]) & (present[:, None, :] > 0)
    ids = jnp.sum(jnp.where(match, place[None, None, :], 0), axis=2)
    position = (rank + CAP * jnp.arange(N_COL, dtype=jnp.int32)[:, None]).reshape(-1)
    rowc = jnp.sum(jnp.where(hits, position[None, :], 0), axis=1)
    return ids, rowc


def per_device(tiles, tile_row, tile_col, tile_count, vectors):
    bf16, f32 = jnp.bfloat16, jnp.float32
    shape = jax.ShapeDtypeStruct
    local = tiles[0, 0]
    rows, cols, live = tile_row[0, 0], tile_col[0, 0], tile_count[0, 0]
    row_at = lax.axis_index("row")
    x, core = row_at // 2, row_at % 2

    def along_x(value, d):
        return lax.ppermute(value, "row", [(i, (i + 2 * d) % 8) for i in range(8)])

    def swap_core(value):
        return lax.ppermute(value, "row", [(i, i ^ 1) for i in range(8)])

    mine = vectors.reshape(K, SHARE * TILE)
    near = [mine, along_x(mine, -1), along_x(mine, 1)]

    ids, rowc = named_rows(rows)
    codes, counts = slot_lists(rowc, cols, live, x)
    scal = jnp.stack([live, x, core, counts[0], counts[1]]).astype(jnp.int32)
    near_codes, far_codes = codes[0], codes[1]
    lanes = jnp.pad(ids, ((0, 0), (0, TILE - CAP))).astype(bf16)
    id_rows = jnp.broadcast_to(lanes[:, None, :], (N_COL, 16, TILE))
    near, near_codes, far_codes, id_rows, scal = lax.optimization_barrier(
        (near, near_codes, far_codes, id_rows, scal)
    )

    far = along_x(near[1], -1)
    begun, held = call(
        forward_near_kernel,
        [shape((N_NAMED + 1, K, TILE), f32), shape(local.shape, bf16)],
        [near_codes, scal],
        [pltpu.with_memory_space_constraint(local, pltpu.HBM)] + near + [swap_core(v) for v in near],
        [
            pltpu.VMEM((2 * N_X * SHARE, K, TILE), bf16),
            pltpu.SemaphoreType.DMA((local.shape[0] // CHUNK,)),
        ],
        hbm=(0,),
    )
    far, begun = lax.optimization_barrier((far, begun))
    send, _ = call(
        forward_far_kernel,
        [shape((N_COL, PAY_ROWS, TILE), bf16), shape((N_NAMED + 1, K, TILE), f32)],
        [far_codes, scal],
        [held, id_rows, far, swap_core(far), begun],
        [pltpu.VMEM((2 * SHARE, K, TILE), bf16)],
        aliases={6: 1},
    )
    recv = lax.all_to_all(send, "col", 0, 0, tiled=True)
    image, spread = call(
        reduce_kernel,
        [shape((K, SHARE * TILE), bf16), shape((N_COL, RUN_ROWS, TILE), bf16)],
        [],
        [recv],
        [
            pltpu.VMEM((SHARE, K, TILE), f32),
            pltpu.VMEM((SHARE, K, TILE), bf16),
            pltpu.VMEM((N_COL, TILE), jnp.int32),
            pltpu.SMEM((N_COL, TILE), jnp.int32),
            pltpu.SemaphoreType.DMA,
        ],
    )
    named = lax.all_to_all(spread, "col", 0, 0, tiled=True).reshape(N_NAMED, K, TILE)

    block = (SHARE, K, TILE)
    wide, narrow = shape(block, f32), shape(block, bf16)
    keep, give = call(
        backward_near_kernel,
        [shape((3,) + block, f32), shape((3,) + block, bf16)],
        [near_codes, scal],
        [held, named],
        [pltpu.VMEM((2 * N_X * SHARE + 1, K, TILE), f32)],
    )
    own, one, three = call(near_pair_kernel, [wide, narrow, narrow], [], [keep, swap_core(give)])
    one, three, named = lax.optimization_barrier((one, three, named))
    one, three = along_x(one, 1), along_x(three, -1)
    keep, *gives = call(
        backward_far_kernel,
        [wide] + [shape((SHARE // PARTS, K, TILE), bf16)] * PARTS,
        [far_codes, scal],
        [held, named],
        [pltpu.VMEM((2 * SHARE + 1, K, TILE), f32)],
        cost=LONG,
    )
    away = call(far_pair_kernel, narrow, [], [keep] + [swap_core(v) for v in gives])
    two = along_x(away, 2)
    begun = call(near_sum_kernel, wide, [], [own, one, three], cost=LONG)
    back = call(final_kernel, shape((K, SHARE * TILE), bf16), [], [begun, two])
    return image, back.reshape(vectors.shape)


def solution(mesh):
    return jax.shard_map(
        per_device,
        mesh=mesh,
        in_specs=(
            P("row", "col", None, None, None),
            P("row", "col", None),
            P("row", "col", None),
            P("row", "col"),
            P(None, "row", "col", None),
        ),
        out_specs=(P(None, ("row", "col")), P(None, "row", "col", None)),
        check_vma=False,
    )
```

```python
import jax
import jax.numpy as jnp
from jax import lax
from jax.experimental import pallas as pl
from jax.experimental.pallas import tpu as pltpu
from jax.sharding import PartitionSpec as P

TILE = 128
K = 32
SHARE = 32
CAP = 12
N_COL = 16
N_X = 4
RUN_ROWS = CAP * K
PAY_ROWS = RUN_ROWS + 16
N_NAMED = N_COL * CAP
GROUP = 32
CHUNK = 32
NEAR = (0, 1, 3)
PARTS = 2
LONG = pl.CostEstimate(flops=1 << 36, transcendentals=0, bytes_accessed=1 << 26)


def tile_copy(tiles, held, sems, chunk):
    span = pl.ds(pl.multiple_of(chunk * CHUNK, CHUNK), CHUNK)
    return pltpu.make_async_copy(tiles.at[span], held.at[span], sems.at[chunk])


def in_hbm(value):
    return pltpu.with_memory_space_constraint(value, pltpu.HBM)


def code_parts(code):
    return code & 511, (code >> 9) & 255, (code >> 17) & 255, code >> 25


def sweep(count, codes, tiles, left, total, spots, dims, ready=None):
    def group(g, seen):
        base = g * GROUP
        if ready is not None:
            seen = ready(seen, (codes[jnp.minimum(base + GROUP, count) - 1] & 511) // CHUNK + 1)
        slots, sources, places = zip(*(spots(*code_parts(codes[base + u])) for u in range(GROUP)))
        blank = jnp.zeros((K, TILE), jnp.bfloat16)
        products = []
        for u in range(0, GROUP, 2):
            above = jnp.concatenate([left[sources[u]], blank], axis=1)
            below = jnp.concatenate([blank, left[sources[u + 1]]], axis=1)
            pair = lax.dot_general(
                jnp.concatenate([above, below], axis=0),
                jnp.concatenate([tiles[slots[u]], tiles[slots[u + 1]]], axis=dims),
                (((1,), (dims,)), ((), ())),
                preferred_element_type=jnp.float32,
            )
            products += [pair[:K], pair[K:]]
        for place, product in zip(places, products):
            total[place] += product
        return seen

    return lax.fori_loop(0, (count + GROUP - 1) // GROUP, group, 0)


def clear_blocks(total, count):
    def clear(p, _):
        total[p] = jnp.zeros((K, TILE), jnp.float32)
        return 0

    lax.fori_loop(0, count, clear, 0, unroll=8)


def forward_spots(blocks):
    return lambda slot, row, col, spare: (slot, col & (blocks - 1), row + N_NAMED * spare)


def forward_near_kernel(codes, scal, tiles, *refs):
    mine_hbm, (total, held, vec, sems, mine, sem) = refs[0], refs[6:]
    pieces = (mine,) + refs[1:6]
    live, x, core = scal[0], scal[1], scal[2]
    chunks = (live + CHUNK - 1) // CHUNK

    def start(chunk, _):
        tile_copy(tiles, held, sems, chunk).start()
        return 0

    def wait(chunk, _):
        tile_copy(tiles, held, sems, chunk).wait()
        return 0

    def ready(seen, need):
        lax.fori_loop(seen, need, wait, 0)
        return jnp.maximum(seen, need)

    fetch = pltpu.make_async_copy(mine_hbm, mine, sem)
    fetch.start()
    lax.fori_loop(0, chunks, start, 0)
    clear_blocks(total, N_NAMED)
    fetch.wait()
    for i, d in enumerate(NEAR):
        for other in range(2):
            piece = pieces[i + 3 * other]
            first = (((x + d) % N_X) * 2 + (core + other) % 2) * SHARE
            for b in range(SHARE):
                vec[first + b] = piece[:, b * TILE:(b + 1) * TILE]
    seen = sweep(scal[3], codes, held, vec, total, forward_spots(2 * N_X * SHARE), 1, ready)
    lax.fori_loop(seen, chunks, wait, 0)


def forward_far_kernel(codes, scal, tiles, ids, here, there, begun, send, total, vec):
    core = scal[2]
    for other, piece in enumerate((here, there)):
        first = ((core + other) % 2) * SHARE
        for b in range(SHARE):
            vec[first + b] = piece[:, b * TILE:(b + 1) * TILE]
    sweep(scal[4], codes, tiles, vec, total, forward_spots(2 * SHARE), 1)

    def pack(c, _):
        for q in range(CAP):
            send[c, q * K:(q + 1) * K] = total[c * CAP + q].astype(jnp.bfloat16)
        send[c, RUN_ROWS:] = ids[c]
        return 0

    lax.fori_loop(0, N_COL, pack, 0)


def reduce_kernel(recv, image, send, total, blocks, wide_ids, ids, sem):
    for c in range(N_COL):
        wide_ids[c:c + 1] = recv[c, RUN_ROWS:][0:1].astype(jnp.float32).astype(jnp.int32)
    copy = pltpu.make_async_copy(wide_ids, ids, sem)
    copy.start()
    for b in range(SHARE):
        total[b] = jnp.zeros((K, TILE), jnp.float32)
    copy.wait()

    def add(c, _):
        for q in range(CAP):
            total[ids[c, q]] += recv[c, q * K:(q + 1) * K].astype(jnp.float32)
        return 0

    lax.fori_loop(0, N_COL, add, 0)
    for b in range(SHARE):
        block = total[b].astype(jnp.bfloat16)
        blocks[b] = block
        image[:, b * TILE:(b + 1) * TILE] = block

    def spread(c, _):
        for q in range(CAP):
            send[c, q * K:(q + 1) * K] = blocks[ids[c, q]]
        return 0

    lax.fori_loop(0, N_COL, spread, 0)


def backward_spots(blocks):
    return lambda slot, row, col, spare: (slot, row, (col & (blocks - 1)) + blocks * spare)


def backward_near_kernel(codes, scal, tiles, recv, keep, give, total):
    x, core = scal[1], scal[2]
    for d in NEAR:
        clear_blocks(total.at[pl.ds(((x + d) % N_X) * 2 * SHARE, 2 * SHARE)], 2 * SHARE)
    sweep(scal[3], codes, tiles, recv, total, backward_spots(2 * N_X * SHARE), 0)

    def split(b, _):
        for i, d in enumerate(NEAR):
            first = ((x + d) % N_X) * 2 * SHARE + b
            keep[i, b] = total[first + core * SHARE]
            give[i, b] = total[first + (1 - core) * SHARE].astype(give.dtype)
        return 0

    lax.fori_loop(0, SHARE, split, 0, unroll=4)


def backward_far_kernel(codes, scal, tiles, recv, keep, *rest):
    gives, total = rest[:-1], rest[-1]
    core = scal[2]
    clear_blocks(total, 2 * SHARE)
    sweep(scal[4], codes, tiles, recv, total, backward_spots(2 * SHARE), 0)
    part = SHARE // len(gives)

    def split(b, _):
        for i, give in enumerate(gives):
            keep[i * part + b] = total[core * SHARE + i * part + b]
            give[b] = total[(1 - core) * SHARE + i * part + b].astype(give.dtype)
        return 0

    lax.fori_loop(0, part, split, 0, unroll=2)


def near_pair_kernel(keep, got, own, one, three):
    def step(b, _):
        for i, out in enumerate((own, one, three)):
            out[b] = (keep[i, b] + got[i, b].astype(jnp.float32)).astype(out.dtype)
        return 0

    lax.fori_loop(0, SHARE, step, 0, unroll=4)


def far_pair_kernel(keep, *rest):
    gots, out = rest[:-1], rest[-1]
    part = SHARE // len(gots)

    def step(b, _):
        for i, got in enumerate(gots):
            out[i * part + b] = (keep[i * part + b] + got[b].astype(jnp.float32)).astype(out.dtype)
        return 0

    lax.fori_loop(0, part, step, 0, unroll=2)


def near_sum_kernel(own, one, three, out):
    def step(b, _):
        out[b] = own[b] + one[b].astype(jnp.float32) + three[b].astype(jnp.float32)
        return 0

    lax.fori_loop(0, SHARE, step, 0, unroll=4)


def final_kernel(begun, two, out):
    for b in range(SHARE):
        total = begun[b] + two[b].astype(jnp.float32)
        out[:, b * TILE:(b + 1) * TILE] = total.astype(jnp.bfloat16)


def call(kernel, outs, scalars, arrays, scratch=(), limit=8, hbm=(), aliases=None, cost=None):
    spec_vmem = pl.BlockSpec(memory_space=pltpu.VMEM)
    spec_smem = pl.BlockSpec(memory_space=pltpu.SMEM)
    spec_hbm = pl.BlockSpec(memory_space=pltpu.HBM)
    specs = [spec_smem] * len(scalars)
    specs += [spec_hbm if i in hbm else spec_vmem for i in range(len(arrays))]
    single = not isinstance(outs, (list, tuple))
    return pl.pallas_call(
        kernel,
        out_shape=outs,
        in_specs=specs,
        out_specs=spec_vmem if single else [spec_vmem] * len(outs),
        scratch_shapes=list(scratch),
        input_output_aliases=aliases or {},
        cost_estimate=cost,
        compiler_params=pltpu.CompilerParams(vmem_limit_bytes=limit << 20),
    )(*scalars, *arrays)


def slot_lists(rowc, cols, live, x):
    slot = jnp.arange(rowc.shape[0], dtype=jnp.int32)
    code = slot | (rowc << 9) | (cols << 17)
    far = (((cols >> 6) - x) & (N_X - 1)) == 2
    member = jnp.stack([(slot < live) & ~far, (slot < live) & far])
    earlier = slot[:, None] < slot[None, :]
    place = jnp.sum(jnp.where(member[:, :, None] & earlier[None], 1, 0), axis=1)
    match = member[:, :, None] & (place[:, :, None] == slot[None, None, :])
    packed = jnp.sum(jnp.where(match, code[None, :, None], 0), axis=1)
    counts = jnp.sum(member.astype(jnp.int32), axis=1)
    return jnp.where(slot[None, :] < counts[:, None], packed, 1 << 25), counts


def named_rows(rows):
    hits = rows[:, None] == jnp.arange(N_COL * SHARE, dtype=jnp.int32)[None, :]
    present = jnp.any(hits, axis=0).astype(jnp.int32).reshape(N_COL, SHARE)
    place = jnp.arange(SHARE, dtype=jnp.int32)
    rank = jnp.sum(jnp.where(place[:, None] < place[None, :], present[:, :, None], 0), axis=1)
    match = (rank[:, None, :] == jnp.arange(CAP, dtype=jnp.int32)[None, :, None]) & (present[:, None, :] > 0)
    ids = jnp.sum(jnp.where(match, place[None, None, :], 0), axis=2)
    position = (rank + CAP * jnp.arange(N_COL, dtype=jnp.int32)[:, None]).reshape(-1)
    rowc = jnp.sum(jnp.where(hits, position[None, :], 0), axis=1)
    return ids, rowc


def per_device(tiles, tile_row, tile_col, tile_count, vectors):
    bf16, f32 = jnp.bfloat16, jnp.float32
    shape = jax.ShapeDtypeStruct
    local = tiles[0, 0]
    rows, cols, live = tile_row[0, 0], tile_col[0, 0], tile_count[0, 0]
    row_at = lax.axis_index("row")
    x, core = row_at // 2, row_at % 2

    def along_x(value, d):
        return lax.ppermute(value, "row", [(i, (i + 2 * d) % 8) for i in range(8)])

    def swap_core(value):
        return lax.ppermute(value, "row", [(i, i ^ 1) for i in range(8)])

    mine = vectors.reshape(K, SHARE * TILE)
    near = [mine, along_x(mine, -1), along_x(mine, 1)]

    ids, rowc = named_rows(rows)
    codes, counts = slot_lists(rowc, cols, live, x)
    scal = jnp.stack([live, x, core, counts[0], counts[1]]).astype(jnp.int32)
    near_codes, far_codes = codes[0], codes[1]
    lanes = jnp.pad(ids, ((0, 0), (0, TILE - CAP))).astype(bf16)
    id_rows = jnp.broadcast_to(lanes[:, None, :], (N_COL, 16, TILE))
    near, near_codes, far_codes, id_rows, scal = lax.optimization_barrier(
        (near, near_codes, far_codes, id_rows, scal)
    )

    swapped = [swap_core(v) for v in near]
    far = along_x(near[1], -1)
    begun, held = call(
        forward_near_kernel,
        [shape((N_NAMED + 1, K, TILE), f32), shape(local.shape, bf16)],
        [near_codes, scal],
        [in_hbm(local), in_hbm(mine)] + near[1:] + swapped,
        [
            pltpu.VMEM((2 * N_X * SHARE, K, TILE), bf16),
            pltpu.SemaphoreType.DMA((local.shape[0] // CHUNK,)),
            pltpu.VMEM((K, SHARE * TILE), bf16),
            pltpu.SemaphoreType.DMA,
        ],
        hbm=(0, 1),
    )
    far, far_there, begun = lax.optimization_barrier((far, along_x(swapped[2], 1), begun))
    send, _ = call(
        forward_far_kernel,
        [shape((N_COL, PAY_ROWS, TILE), bf16), shape((N_NAMED + 1, K, TILE), f32)],
        [far_codes, scal],
        [held, id_rows, far, far_there, begun],
        [pltpu.VMEM((2 * SHARE, K, TILE), bf16)],
        aliases={6: 1},
    )
    recv = lax.all_to_all(send, "col", 0, 0, tiled=True)
    image, spread = call(
        reduce_kernel,
        [shape((K, SHARE * TILE), bf16), shape((N_COL, RUN_ROWS, TILE), bf16)],
        [],
        [recv],
        [
            pltpu.VMEM((SHARE, K, TILE), f32),
            pltpu.VMEM((SHARE, K, TILE), bf16),
            pltpu.VMEM((N_COL, TILE), jnp.int32),
            pltpu.SMEM((N_COL, TILE), jnp.int32),
            pltpu.SemaphoreType.DMA,
        ],
    )
    named = lax.all_to_all(spread, "col", 0, 0, tiled=True).reshape(N_NAMED, K, TILE)

    block = (SHARE, K, TILE)
    wide, narrow = shape(block, f32), shape(block, bf16)
    keep, give = call(
        backward_near_kernel,
        [shape((3,) + block, f32), shape((3,) + block, bf16)],
        [near_codes, scal],
        [held, named],
        [pltpu.VMEM((2 * N_X * SHARE + 1, K, TILE), f32)],
    )
    own, one, three = call(near_pair_kernel, [wide, narrow, narrow], [], [keep, swap_core(give)])
    one, three, named = lax.optimization_barrier((one, three, named))
    one, three = along_x(one, 1), along_x(three, -1)
    keep, *gives = call(
        backward_far_kernel,
        [wide] + [shape((SHARE // PARTS, K, TILE), bf16)] * PARTS,
        [far_codes, scal],
        [held, named],
        [pltpu.VMEM((2 * SHARE + 1, K, TILE), f32)],
        cost=LONG,
    )
    away = call(far_pair_kernel, narrow, [], [keep] + [swap_core(v) for v in gives])
    two = along_x(away, 2)
    begun = call(near_sum_kernel, wide, [], [own, one, three], cost=LONG)
    back = call(final_kernel, shape((K, SHARE * TILE), bf16), [], [begun, two])
    return image, back.reshape(vectors.shape)


def solution(mesh):
    return jax.shard_map(
        per_device,
        mesh=mesh,
        in_specs=(
            P("row", "col", None, None, None),
            P("row", "col", None),
            P("row", "col", None),
            P("row", "col"),
            P(None, "row", "col", None),
        ),
        out_specs=(P(None, ("row", "col")), P(None, "row", "col", None)),
        check_vma=False,
    )
```

```python
import jax
import jax.numpy as jnp
from jax import lax
from jax.experimental import pallas as pl
from jax.experimental.pallas import tpu as pltpu
from jax.sharding import PartitionSpec as P

TILE = 128
K = 32
SHARE = 32
CAP = 12
N_COL = 16
N_X = 4
RUN_ROWS = CAP * K
PAY_ROWS = RUN_ROWS + 8
N_NAMED = N_COL * CAP
GROUP = 32
CHUNK = 32
NEAR = (0, 1, 3)
PARTS = 2
LONG = pl.CostEstimate(flops=1 << 36, transcendentals=0, bytes_accessed=1 << 26)


def tile_copy(tiles, held, sems, chunk):
    span = pl.ds(pl.multiple_of(chunk * CHUNK, CHUNK), CHUNK)
    return pltpu.make_async_copy(tiles.at[span], held.at[span], sems.at[chunk])


def in_hbm(value):
    return pltpu.with_memory_space_constraint(value, pltpu.HBM)


def image_kernel(blocks, image):
    for b in range(SHARE):
        image[:, b * TILE:(b + 1) * TILE] = blocks[b]


def code_parts(code):
    return code & 511, (code >> 9) & 255, (code >> 17) & 255, code >> 25


def sweep(count, codes, tiles, left, total, spots, dims, ready=None):
    def group(g, seen):
        base = g * GROUP
        if ready is not None:
            seen = ready(seen, (codes[jnp.minimum(base + GROUP, count) - 1] & 511) // CHUNK + 1)
        slots, sources, places = zip(*(spots(*code_parts(codes[base + u])) for u in range(GROUP)))
        blank = jnp.zeros((K, TILE), jnp.bfloat16)
        products = []
        for u in range(0, GROUP, 2):
            above = jnp.concatenate([left[sources[u]], blank], axis=1)
            below = jnp.concatenate([blank, left[sources[u + 1]]], axis=1)
            pair = lax.dot_general(
                jnp.concatenate([above, below], axis=0),
                jnp.concatenate([tiles[slots[u]], tiles[slots[u + 1]]], axis=dims),
                (((1,), (dims,)), ((), ())),
                preferred_element_type=jnp.float32,
            )
            products += [pair[:K], pair[K:]]
        for place, product in zip(places, products):
            total[place] += product
        return seen

    return lax.fori_loop(0, (count + GROUP - 1) // GROUP, group, 0)


def clear_blocks(total, count):
    def clear(p, _):
        total[p] = jnp.zeros((K, TILE), jnp.float32)
        return 0

    lax.fori_loop(0, count, clear, 0, unroll=8)


def forward_spots(blocks):
    return lambda slot, row, col, spare: (slot, col & (blocks - 1), row + N_NAMED * spare)


def forward_near_kernel(codes, scal, tiles, *refs):
    mine_hbm, (total, held, vec, sems, mine, sem) = refs[0], refs[6:]
    pieces = (mine,) + refs[1:6]
    live, x, core = scal[0], scal[1], scal[2]
    chunks = (live + CHUNK - 1) // CHUNK

    def start(chunk, _):
        tile_copy(tiles, held, sems, chunk).start()
        return 0

    def wait(chunk, _):
        tile_copy(tiles, held, sems, chunk).wait()
        return 0

    def ready(seen, need):
        lax.fori_loop(seen, need, wait, 0)
        return jnp.maximum(seen, need)

    fetch = pltpu.make_async_copy(mine_hbm, mine, sem)
    fetch.start()
    lax.fori_loop(0, chunks, start, 0)
    clear_blocks(total, N_NAMED)
    fetch.wait()
    for i, d in enumerate(NEAR):
        for other in range(2):
            piece = pieces[i + 3 * other]
            first = (((x + d) % N_X) * 2 + (core + other) % 2) * SHARE
            for b in range(SHARE):
                vec[first + b] = piece[:, b * TILE:(b + 1) * TILE]
    seen = sweep(scal[3], codes, held, vec, total, forward_spots(2 * N_X * SHARE), 1, ready)
    lax.fori_loop(seen, chunks, wait, 0)


def forward_far_kernel(codes, scal, tiles, ids, here, there, begun, send, total, vec):
    core = scal[2]
    for other, piece in enumerate((here, there)):
        first = ((core + other) % 2) * SHARE
        for b in range(SHARE):
            vec[first + b] = piece[:, b * TILE:(b + 1) * TILE]
    sweep(scal[4], codes, tiles, vec, total, forward_spots(2 * SHARE), 1)

    def pack(c, _):
        for q in range(CAP):
            send[c, q * K:(q + 1) * K] = total[c * CAP + q].astype(jnp.bfloat16)
        send[c, RUN_ROWS:] = ids[c]
        return 0

    lax.fori_loop(0, N_COL, pack, 0)


def reduce_kernel(recv, blocks, send, total, wide_ids, ids, sem):
    for c in range(N_COL):
        wide_ids[c:c + 1] = recv[c, RUN_ROWS:][0:1].astype(jnp.float32).astype(jnp.int32)
    copy = pltpu.make_async_copy(wide_ids, ids, sem)
    copy.start()
    for b in range(SHARE):
        total[b] = jnp.zeros((K, TILE), jnp.float32)
    copy.wait()

    def add(c, _):
        spots = [ids[c, q] for q in range(CAP)]
        sums = [total[p] + recv[c, q * K:(q + 1) * K].astype(jnp.float32) for q, p in enumerate(spots)]
        for p, value in zip(spots, sums):
            total[p] = value
        return 0

    lax.fori_loop(0, N_COL, add, 0)
    for b in range(SHARE):
        blocks[b] = total[b].astype(jnp.bfloat16)

    def spread(c, _):
        for q in range(CAP):
            send[c, q * K:(q + 1) * K] = blocks[ids[c, q]]
        return 0

    lax.fori_loop(0, N_COL, spread, 0, unroll=4)


def backward_spots(blocks):
    return lambda slot, row, col, spare: (slot, row, (col & (blocks - 1)) + blocks * spare)


def backward_near_kernel(codes, scal, tiles, recv, keep, give, total):
    x, core = scal[1], scal[2]
    for d in NEAR:
        clear_blocks(total.at[pl.ds(((x + d) % N_X) * 2 * SHARE, 2 * SHARE)], 2 * SHARE)
    sweep(scal[3], codes, tiles, recv, total, backward_spots(2 * N_X * SHARE), 0)

    def split(b, _):
        for i, d in enumerate(NEAR):
            first = ((x + d) % N_X) * 2 * SHARE + b
            keep[i, b] = total[first + core * SHARE]
            give[i, b] = total[first + (1 - core) * SHARE].astype(give.dtype)
        return 0

    lax.fori_loop(0, SHARE, split, 0, unroll=4)


def backward_far_kernel(codes, scal, tiles, recv, keep, *rest):
    gives, total = rest[:-1], rest[-1]
    core = scal[2]
    clear_blocks(total, 2 * SHARE)
    sweep(scal[4], codes, tiles, recv, total, backward_spots(2 * SHARE), 0)
    part = SHARE // len(gives)

    def split(b, _):
        for i, give in enumerate(gives):
            keep[i * part + b] = total[core * SHARE + i * part + b]
            give[b] = total[(1 - core) * SHARE + i * part + b].astype(give.dtype)
        return 0

    lax.fori_loop(0, part, split, 0, unroll=2)


def near_pair_kernel(keep, got, own, one, three):
    def step(b, _):
        for i, out in enumerate((own, one, three)):
            out[b] = (keep[i, b] + got[i, b].astype(jnp.float32)).astype(out.dtype)
        return 0

    lax.fori_loop(0, SHARE, step, 0, unroll=4)


def far_pair_kernel(keep, *rest):
    gots, out = rest[:-1], rest[-1]
    part = SHARE // len(gots)

    def step(b, _):
        for i, got in enumerate(gots):
            out[i * part + b] = (keep[i * part + b] + got[b].astype(jnp.float32)).astype(out.dtype)
        return 0

    lax.fori_loop(0, part, step, 0, unroll=2)


def near_sum_kernel(own, one, three, out):
    def step(b, _):
        out[b] = own[b] + one[b].astype(jnp.float32) + three[b].astype(jnp.float32)
        return 0

    lax.fori_loop(0, SHARE, step, 0, unroll=4)


def final_kernel(begun, two, out):
    for b in range(SHARE):
        total = begun[b] + two[b].astype(jnp.float32)
        out[:, b * TILE:(b + 1) * TILE] = total.astype(jnp.bfloat16)


def call(kernel, outs, scalars, arrays, scratch=(), limit=8, hbm=(), aliases=None, cost=None):
    spec_vmem = pl.BlockSpec(memory_space=pltpu.VMEM)
    spec_smem = pl.BlockSpec(memory_space=pltpu.SMEM)
    spec_hbm = pl.BlockSpec(memory_space=pltpu.HBM)
    specs = [spec_smem] * len(scalars)
    specs += [spec_hbm if i in hbm else spec_vmem for i in range(len(arrays))]
    single = not isinstance(outs, (list, tuple))
    return pl.pallas_call(
        kernel,
        out_shape=outs,
        in_specs=specs,
        out_specs=spec_vmem if single else [spec_vmem] * len(outs),
        scratch_shapes=list(scratch),
        input_output_aliases=aliases or {},
        cost_estimate=cost,
        compiler_params=pltpu.CompilerParams(vmem_limit_bytes=limit << 20),
    )(*scalars, *arrays)


def slot_lists(rowc, cols, live, x):
    slot = jnp.arange(rowc.shape[0], dtype=jnp.int32)
    code = slot | (rowc << 9) | (cols << 17)
    far = (((cols >> 6) - x) & (N_X - 1)) == 2
    member = jnp.stack([(slot < live) & ~far, (slot < live) & far])
    earlier = slot[:, None] < slot[None, :]
    place = jnp.sum(jnp.where(member[:, :, None] & earlier[None], 1, 0), axis=1)
    match = member[:, :, None] & (place[:, :, None] == slot[None, None, :])
    packed = jnp.sum(jnp.where(match, code[None, :, None], 0), axis=1)
    counts = jnp.sum(member.astype(jnp.int32), axis=1)
    return jnp.where(slot[None, :] < counts[:, None], packed, 1 << 25), counts


def named_rows(rows):
    hits = rows[:, None] == jnp.arange(N_COL * SHARE, dtype=jnp.int32)[None, :]
    present = jnp.any(hits, axis=0).astype(jnp.int32).reshape(N_COL, SHARE)
    place = jnp.arange(SHARE, dtype=jnp.int32)
    rank = jnp.sum(jnp.where(place[:, None] < place[None, :], present[:, :, None], 0), axis=1)
    match = (rank[:, None, :] == jnp.arange(CAP, dtype=jnp.int32)[None, :, None]) & (present[:, None, :] > 0)
    ids = jnp.sum(jnp.where(match, place[None, None, :], 0), axis=2)
    position = (rank + CAP * jnp.arange(N_COL, dtype=jnp.int32)[:, None]).reshape(-1)
    rowc = jnp.sum(jnp.where(hits, position[None, :], 0), axis=1)
    return ids, rowc


def per_device(tiles, tile_row, tile_col, tile_count, vectors):
    bf16, f32 = jnp.bfloat16, jnp.float32
    shape = jax.ShapeDtypeStruct
    local = tiles[0, 0]
    rows, cols, live = tile_row[0, 0], tile_col[0, 0], tile_count[0, 0]
    row_at = lax.axis_index("row")
    x, core = row_at // 2, row_at % 2

    def along_x(value, d):
        return lax.ppermute(value, "row", [(i, (i + 2 * d) % 8) for i in range(8)])

    def swap_core(value):
        return lax.ppermute(value, "row", [(i, i ^ 1) for i in range(8)])

    mine = vectors.reshape(K, SHARE * TILE)
    near = [mine, along_x(mine, -1), along_x(mine, 1)]

    ids, rowc = named_rows(rows)
    codes, counts = slot_lists(rowc, cols, live, x)
    scal = jnp.stack([live, x, core, counts[0], counts[1]]).astype(jnp.int32)
    near_codes, far_codes = codes[0], codes[1]
    lanes = jnp.pad(ids, ((0, 0), (0, TILE - CAP))).astype(bf16)
    id_rows = jnp.broadcast_to(lanes[:, None, :], (N_COL, 8, TILE))
    near, near_codes, far_codes, id_rows, scal = lax.optimization_barrier(
        (near, near_codes, far_codes, id_rows, scal)
    )

    swapped = [swap_core(v) for v in near]
    far = along_x(near[1], -1)
    begun, held = call(
        forward_near_kernel,
        [shape((N_NAMED + 1, K, TILE), f32), shape(local.shape, bf16)],
        [near_codes, scal],
        [in_hbm(local), in_hbm(mine)] + near[1:] + swapped,
        [
            pltpu.VMEM((2 * N_X * SHARE, K, TILE), bf16),
            pltpu.SemaphoreType.DMA((local.shape[0] // CHUNK,)),
            pltpu.VMEM((K, SHARE * TILE), bf16),
            pltpu.SemaphoreType.DMA,
        ],
        hbm=(0, 1),
    )
    far, far_there, begun = lax.optimization_barrier((far, along_x(swapped[2], 1), begun))
    send, _ = call(
        forward_far_kernel,
        [shape((N_COL, PAY_ROWS, TILE), bf16), shape((N_NAMED + 1, K, TILE), f32)],
        [far_codes, scal],
        [held, id_rows, far, far_there, begun],
        [pltpu.VMEM((2 * SHARE, K, TILE), bf16)],
        aliases={6: 1},
    )
    recv = lax.all_to_all(send, "col", 0, 0, tiled=True)
    blocks, spread = call(
        reduce_kernel,
        [shape((SHARE, K, TILE), bf16), shape((N_COL, RUN_ROWS, TILE), bf16)],
        [],
        [recv],
        [
            pltpu.VMEM((SHARE, K, TILE), f32),
            pltpu.VMEM((N_COL, TILE), jnp.int32),
            pltpu.SMEM((N_COL, TILE), jnp.int32),
            pltpu.SemaphoreType.DMA,
        ],
    )
    image = call(image_kernel, shape((K, SHARE * TILE), bf16), [], [blocks])
    named = lax.all_to_all(spread, "col", 0, 0, tiled=True).reshape(N_NAMED, K, TILE)

    block = (SHARE, K, TILE)
    wide, narrow = shape(block, f32), shape(block, bf16)
    keep, give = call(
        backward_near_kernel,
        [shape((3,) + block, f32), shape((3,) + block, bf16)],
        [near_codes, scal],
        [held, named],
        [pltpu.VMEM((2 * N_X * SHARE + 1, K, TILE), f32)],
    )
    own, one, three = call(near_pair_kernel, [wide, narrow, narrow], [], [keep, swap_core(give)])
    one, three, named = lax.optimization_barrier((one, three, named))
    one, three = along_x(one, 1), along_x(three, -1)
    keep, *gives = call(
        backward_far_kernel,
        [wide] + [shape((SHARE // PARTS, K, TILE), bf16)] * PARTS,
        [far_codes, scal],
        [held, named],
        [pltpu.VMEM((2 * SHARE + 1, K, TILE), f32)],
        cost=LONG,
    )
    away = call(far_pair_kernel, narrow, [], [keep] + [swap_core(v) for v in gives])
    two = along_x(away, 2)
    begun = call(near_sum_kernel, wide, [], [own, one, three], cost=LONG)
    back = call(final_kernel, shape((K, SHARE * TILE), bf16), [], [begun, two])
    return image, back.reshape(vectors.shape)


def solution(mesh):
    return jax.shard_map(
        per_device,
        mesh=mesh,
        in_specs=(
            P("row", "col", None, None, None),
            P("row", "col", None),
            P("row", "col", None),
            P("row", "col"),
            P(None, "row", "col", None),
        ),
        out_specs=(P(None, ("row", "col")), P(None, "row", "col", None)),
        check_vma=False,
    )
```

```python
import jax
import jax.numpy as jnp
from jax import lax
from jax.experimental import pallas as pl
from jax.experimental.pallas import tpu as pltpu
from jax.sharding import PartitionSpec as P

TILE = 128
K = 32
SHARE = 32
CAP = 12
N_COL = 16
N_X = 4
RUN_ROWS = CAP * K
PAY_ROWS = RUN_ROWS + 8
N_NAMED = N_COL * CAP
GROUP = 32
CHUNK = 32
NEAR = (0, 1, 3)
PARTS = 2
LONG = pl.CostEstimate(flops=1 << 36, transcendentals=0, bytes_accessed=1 << 26)


def tile_copy(tiles, held, sems, chunk):
    span = pl.ds(pl.multiple_of(chunk * CHUNK, CHUNK), CHUNK)
    return pltpu.make_async_copy(tiles.at[span], held.at[span], sems.at[chunk])


def in_hbm(value):
    return pltpu.with_memory_space_constraint(value, pltpu.HBM)


def image_kernel(blocks, image):
    for b in range(SHARE):
        image[:, b * TILE:(b + 1) * TILE] = blocks[b]


def code_parts(code):
    return code & 511, (code >> 9) & 255, (code >> 17) & 255, code >> 25


def sweep(count, codes, tiles, left, total, spots, dims, ready=None):
    def group(g, seen):
        base = g * GROUP
        if ready is not None:
            seen = ready(seen, (codes[jnp.minimum(base + GROUP, count) - 1] & 511) // CHUNK + 1)
        slots, sources, places = zip(*(spots(*code_parts(codes[base + u])) for u in range(GROUP)))
        blank = jnp.zeros((K, TILE), jnp.bfloat16)
        products = []
        for u in range(0, GROUP, 2):
            above = jnp.concatenate([left[sources[u]], blank], axis=1)
            below = jnp.concatenate([blank, left[sources[u + 1]]], axis=1)
            pair = lax.dot_general(
                jnp.concatenate([above, below], axis=0),
                jnp.concatenate([tiles[slots[u]], tiles[slots[u + 1]]], axis=dims),
                (((1,), (dims,)), ((), ())),
                preferred_element_type=jnp.float32,
            )
            products += [pair[:K], pair[K:]]
        for place, product in zip(places, products):
            total[place] += product
        return seen

    return lax.fori_loop(0, (count + GROUP - 1) // GROUP, group, 0)


def clear_blocks(total, count):
    def clear(p, _):
        total[p] = jnp.zeros((K, TILE), jnp.float32)
        return 0

    lax.fori_loop(0, count, clear, 0, unroll=8)


def forward_spots(blocks):
    return lambda slot, row, col, spare: (slot, col & (blocks - 1), row + N_NAMED * spare)


def forward_near_kernel(codes, scal, tiles, *refs):
    mine_hbm, (total, held, vec, sems, mine, sem) = refs[0], refs[6:]
    pieces = (mine,) + refs[1:6]
    live, x, core = scal[0], scal[1], scal[2]
    chunks = (live + CHUNK - 1) // CHUNK

    def start(chunk, _):
        tile_copy(tiles, held, sems, chunk).start()
        return 0

    def wait(chunk, _):
        tile_copy(tiles, held, sems, chunk).wait()
        return 0

    def ready(seen, need):
        lax.fori_loop(seen, need, wait, 0)
        return jnp.maximum(seen, need)

    fetch = pltpu.make_async_copy(mine_hbm, mine, sem)
    fetch.start()
    lax.fori_loop(0, chunks, start, 0)
    clear_blocks(total, N_NAMED)

    def load(i, d, other):
        first = (((x + d) % N_X) * 2 + (core + other) % 2) * SHARE
        for b in range(SHARE):
            vec[first + b] = pieces[i + 3 * other][:, b * TILE:(b + 1) * TILE]

    for i, d in enumerate(NEAR):
        for other in range(2):
            if i + other:
                load(i, d, other)
    fetch.wait()
    load(0, 0, 0)
    seen = sweep(scal[3], codes, held, vec, total, forward_spots(2 * N_X * SHARE), 1, ready)
    lax.fori_loop(seen, chunks, wait, 0)


def forward_far_kernel(codes, scal, tiles, ids, here, there, begun, send, total, vec):
    core = scal[2]
    for other, piece in enumerate((here, there)):
        first = ((core + other) % 2) * SHARE
        for b in range(SHARE):
            vec[first + b] = piece[:, b * TILE:(b + 1) * TILE]
    sweep(scal[4], codes, tiles, vec, total, forward_spots(2 * SHARE), 1)

    def pack(c, _):
        for q in range(CAP):
            send[c, q * K:(q + 1) * K] = total[c * CAP + q].astype(jnp.bfloat16)
        send[c, RUN_ROWS:] = ids[c]
        return 0

    lax.fori_loop(0, N_COL, pack, 0, unroll=4)


def reduce_kernel(recv, blocks, send, total, wide_ids, ids, sem):
    for c in range(N_COL):
        wide_ids[c:c + 1] = recv[c, RUN_ROWS:][0:1].astype(jnp.float32).astype(jnp.int32)
    copy = pltpu.make_async_copy(wide_ids, ids, sem)
    copy.start()
    for b in range(SHARE):
        total[b] = jnp.zeros((K, TILE), jnp.float32)
    copy.wait()

    def add(c, _):
        spots = [ids[c, q] for q in range(CAP)]
        sums = [total[p] + recv[c, q * K:(q + 1) * K].astype(jnp.float32) for q, p in enumerate(spots)]
        for p, value in zip(spots, sums):
            total[p] = value
        return 0

    lax.fori_loop(0, N_COL, add, 0)
    for b in range(SHARE):
        blocks[b] = total[b].astype(jnp.bfloat16)

    def spread(c, _):
        for q in range(CAP):
            send[c, q * K:(q + 1) * K] = blocks[ids[c, q]]
        return 0

    lax.fori_loop(0, N_COL, spread, 0, unroll=4)


def backward_spots(blocks):
    return lambda slot, row, col, spare: (slot, row, (col & (blocks - 1)) + blocks * spare)


def backward_near_kernel(codes, scal, tiles, recv, keep, give, give_own, total):
    x, core = scal[1], scal[2]
    for d in NEAR:
        clear_blocks(total.at[pl.ds(((x + d) % N_X) * 2 * SHARE, 2 * SHARE)], 2 * SHARE)
    sweep(scal[3], codes, tiles, recv, total, backward_spots(2 * N_X * SHARE), 0)

    def split(b, _):
        for i, d in enumerate(NEAR):
            first = ((x + d) % N_X) * 2 * SHARE + b
            keep[i, b] = total[first + core * SHARE]
            swap = total[first + (1 - core) * SHARE].astype(give.dtype)
            if i:
                give[i - 1, b] = swap
            else:
                give_own[b] = swap
        return 0

    lax.fori_loop(0, SHARE, split, 0, unroll=4)


def backward_far_kernel(codes, scal, tiles, recv, keep, *rest):
    gives, total = rest[:-1], rest[-1]
    core = scal[2]
    clear_blocks(total, 2 * SHARE)
    sweep(scal[4], codes, tiles, recv, total, backward_spots(2 * SHARE), 0)
    part = SHARE // len(gives)

    def split(b, _):
        for i, give in enumerate(gives):
            keep[i * part + b] = total[core * SHARE + i * part + b]
            give[b] = total[(1 - core) * SHARE + i * part + b].astype(give.dtype)
        return 0

    lax.fori_loop(0, part, split, 0, unroll=2)


def side_pair_kernel(keep, got, one, three):
    def step(b, _):
        for i, out in enumerate((one, three)):
            out[b] = (keep[i + 1, b] + got[i, b].astype(jnp.float32)).astype(out.dtype)
        return 0

    lax.fori_loop(0, SHARE, step, 0, unroll=4)


def far_pair_kernel(keep, *rest):
    gots, out = rest[:-1], rest[-1]
    part = SHARE // len(gots)

    def step(b, _):
        for i, got in enumerate(gots):
            out[i * part + b] = (keep[i * part + b] + got[b].astype(jnp.float32)).astype(out.dtype)
        return 0

    lax.fori_loop(0, part, step, 0, unroll=2)


def near_sum_kernel(keep, got, one, three, out):
    def step(b, _):
        out[b] = (
            keep[0, b]
            + got[b].astype(jnp.float32)
            + one[b].astype(jnp.float32)
            + three[b].astype(jnp.float32)
        )
        return 0

    lax.fori_loop(0, SHARE, step, 0, unroll=4)


def final_kernel(begun, two, out):
    for b in range(SHARE):
        total = begun[b] + two[b].astype(jnp.float32)
        out[:, b * TILE:(b + 1) * TILE] = total.astype(jnp.bfloat16)


def call(kernel, outs, scalars, arrays, scratch=(), limit=8, hbm=(), aliases=None, cost=None):
    spec_vmem = pl.BlockSpec(memory_space=pltpu.VMEM)
    spec_smem = pl.BlockSpec(memory_space=pltpu.SMEM)
    spec_hbm = pl.BlockSpec(memory_space=pltpu.HBM)
    specs = [spec_smem] * len(scalars)
    specs += [spec_hbm if i in hbm else spec_vmem for i in range(len(arrays))]
    single = not isinstance(outs, (list, tuple))
    return pl.pallas_call(
        kernel,
        out_shape=outs,
        in_specs=specs,
        out_specs=spec_vmem if single else [spec_vmem] * len(outs),
        scratch_shapes=list(scratch),
        input_output_aliases=aliases or {},
        cost_estimate=cost,
        compiler_params=pltpu.CompilerParams(vmem_limit_bytes=limit << 20),
    )(*scalars, *arrays)


def slot_lists(rowc, cols, live, x):
    slot = jnp.arange(rowc.shape[0], dtype=jnp.int32)
    code = slot | (rowc << 9) | (cols << 17)
    far = (((cols >> 6) - x) & (N_X - 1)) == 2
    member = jnp.stack([(slot < live) & ~far, (slot < live) & far])
    earlier = slot[:, None] < slot[None, :]
    place = jnp.sum(jnp.where(member[:, :, None] & earlier[None], 1, 0), axis=1)
    match = member[:, :, None] & (place[:, :, None] == slot[None, None, :])
    packed = jnp.sum(jnp.where(match, code[None, :, None], 0), axis=1)
    counts = jnp.sum(member.astype(jnp.int32), axis=1)
    return jnp.where(slot[None, :] < counts[:, None], packed, 1 << 25), counts


def named_rows(rows):
    hits = rows[:, None] == jnp.arange(N_COL * SHARE, dtype=jnp.int32)[None, :]
    present = jnp.any(hits, axis=0).astype(jnp.int32).reshape(N_COL, SHARE)
    place = jnp.arange(SHARE, dtype=jnp.int32)
    rank = jnp.sum(jnp.where(place[:, None] < place[None, :], present[:, :, None], 0), axis=1)
    match = (rank[:, None, :] == jnp.arange(CAP, dtype=jnp.int32)[None, :, None]) & (present[:, None, :] > 0)
    ids = jnp.sum(jnp.where(match, place[None, None, :], 0), axis=2)
    position = (rank + CAP * jnp.arange(N_COL, dtype=jnp.int32)[:, None]).reshape(-1)
    rowc = jnp.sum(jnp.where(hits, position[None, :], 0), axis=1)
    return ids, rowc


def per_device(tiles, tile_row, tile_col, tile_count, vectors):
    bf16, f32 = jnp.bfloat16, jnp.float32
    shape = jax.ShapeDtypeStruct
    local = tiles[0, 0]
    rows, cols, live = tile_row[0, 0], tile_col[0, 0], tile_count[0, 0]
    row_at = lax.axis_index("row")
    x, core = row_at // 2, row_at % 2

    def along_x(value, d):
        return lax.ppermute(value, "row", [(i, (i + 2 * d) % 8) for i in range(8)])

    def swap_core(value):
        return lax.ppermute(value, "row", [(i, i ^ 1) for i in range(8)])

    mine = vectors.reshape(K, SHARE * TILE)
    near = [mine, along_x(mine, -1), along_x(mine, 1)]

    ids, rowc = named_rows(rows)
    codes, counts = slot_lists(rowc, cols, live, x)
    scal = jnp.stack([live, x, core, counts[0], counts[1]]).astype(jnp.int32)
    near_codes, far_codes = codes[0], codes[1]
    lanes = jnp.pad(ids, ((0, 0), (0, TILE - CAP))).astype(bf16)
    id_rows = jnp.broadcast_to(lanes[:, None, :], (N_COL, 8, TILE))
    there = swap_core(mine)
    near, there, near_codes, far_codes, id_rows, scal = lax.optimization_barrier(
        (near, there, near_codes, far_codes, id_rows, scal)
    )

    swapped = [there] + [swap_core(v) for v in near[1:]]
    far = along_x(near[1], -1)
    begun, held = call(
        forward_near_kernel,
        [shape((N_NAMED + 1, K, TILE), f32), shape(local.shape, bf16)],
        [near_codes, scal],
        [in_hbm(local), in_hbm(mine)] + near[1:] + swapped,
        [
            pltpu.VMEM((2 * N_X * SHARE, K, TILE), bf16),
            pltpu.SemaphoreType.DMA((local.shape[0] // CHUNK,)),
            pltpu.VMEM((K, SHARE * TILE), bf16),
            pltpu.SemaphoreType.DMA,
        ],
        hbm=(0, 1),
    )
    far, far_there, begun = lax.optimization_barrier((far, along_x(swapped[2], 1), begun))
    send, _ = call(
        forward_far_kernel,
        [shape((N_COL, PAY_ROWS, TILE), bf16), shape((N_NAMED + 1, K, TILE), f32)],
        [far_codes, scal],
        [held, id_rows, far, far_there, begun],
        [pltpu.VMEM((2 * SHARE, K, TILE), bf16)],
        aliases={6: 1},
    )
    recv = lax.all_to_all(send, "col", 0, 0, tiled=True)
    blocks, spread = call(
        reduce_kernel,
        [shape((SHARE, K, TILE), bf16), shape((N_COL, RUN_ROWS, TILE), bf16)],
        [],
        [recv],
        [
            pltpu.VMEM((SHARE, K, TILE), f32),
            pltpu.VMEM((N_COL, TILE), jnp.int32),
            pltpu.SMEM((N_COL, TILE), jnp.int32),
            pltpu.SemaphoreType.DMA,
        ],
    )
    image = call(image_kernel, shape((K, SHARE * TILE), bf16), [], [blocks])
    named = lax.all_to_all(spread, "col", 0, 0, tiled=True).reshape(N_NAMED, K, TILE)

    block = (SHARE, K, TILE)
    wide, narrow = shape(block, f32), shape(block, bf16)
    near_keep, give, give_own = call(
        backward_near_kernel,
        [shape((3,) + block, f32), shape((2,) + block, bf16), narrow],
        [near_codes, scal],
        [held, named],
        [pltpu.VMEM((2 * N_X * SHARE + 1, K, TILE), f32)],
    )
    one, three = call(side_pair_kernel, [narrow, narrow], [], [near_keep, swap_core(give)])
    one, three, named = lax.optimization_barrier((one, three, named))
    one, three = along_x(one, 1), along_x(three, -1)
    keep, *gives = call(
        backward_far_kernel,
        [wide] + [shape((SHARE // PARTS, K, TILE), bf16)] * PARTS,
        [far_codes, scal],
        [held, named],
        [pltpu.VMEM((2 * SHARE + 1, K, TILE), f32)],
        cost=LONG,
    )
    away = call(far_pair_kernel, narrow, [], [keep] + [swap_core(v) for v in gives])
    two = along_x(away, 2)
    begun = call(near_sum_kernel, wide, [], [near_keep, swap_core(give_own), one, three], cost=LONG)
    back = call(final_kernel, shape((K, SHARE * TILE), bf16), [], [begun, two])
    return image, back.reshape(vectors.shape)


def solution(mesh):
    return jax.shard_map(
        per_device,
        mesh=mesh,
        in_specs=(
            P("row", "col", None, None, None),
            P("row", "col", None),
            P("row", "col", None),
            P("row", "col"),
            P(None, "row", "col", None),
        ),
        out_specs=(P(None, ("row", "col")), P(None, "row", "col", None)),
        check_vma=False,
    )
```

```python
import jax
import jax.numpy as jnp
from jax import lax
from jax.experimental import pallas as pl
from jax.experimental.pallas import tpu as pltpu
from jax.sharding import PartitionSpec as P

TILE = 128
K = 32
SHARE = 32
CAP = 12
N_COL = 16
N_X = 4
RUN_ROWS = CAP * K
PAY_ROWS = RUN_ROWS + 8
N_NAMED = N_COL * CAP
GROUP = 32
CHUNK = 32
NEAR = (0, 1, 3)
PARTS = 2
LONG = pl.CostEstimate(flops=1 << 36, transcendentals=0, bytes_accessed=1 << 26)


def tile_copy(tiles, held, sems, chunk):
    span = pl.ds(pl.multiple_of(chunk * CHUNK, CHUNK), CHUNK)
    return pltpu.make_async_copy(tiles.at[span], held.at[span], sems.at[chunk])


def in_hbm(value):
    return pltpu.with_memory_space_constraint(value, pltpu.HBM)


def image_kernel(blocks, image):
    for b in range(SHARE):
        image[:, b * TILE:(b + 1) * TILE] = blocks[b]


def code_parts(code):
    return code & 511, (code >> 9) & 255, (code >> 17) & 255, code >> 25


def sweep(count, codes, tiles, left, total, spots, dims, ready=None):
    def group(g, seen):
        base = g * GROUP
        if ready is not None:
            seen = ready(seen, (codes[jnp.minimum(base + GROUP, count) - 1] & 511) // CHUNK + 1)
        slots, sources, places = zip(*(spots(*code_parts(codes[base + u])) for u in range(GROUP)))
        blank = jnp.zeros((K, TILE), jnp.bfloat16)
        products = []
        for u in range(0, GROUP, 2):
            above = jnp.concatenate([left[sources[u]], blank], axis=1)
            below = jnp.concatenate([blank, left[sources[u + 1]]], axis=1)
            pair = lax.dot_general(
                jnp.concatenate([above, below], axis=0),
                jnp.concatenate([tiles[slots[u]], tiles[slots[u + 1]]], axis=dims),
                (((1,), (dims,)), ((), ())),
                preferred_element_type=jnp.float32,
            )
            products += [pair[:K], pair[K:]]
        for place, product in zip(places, products):
            total[place] += product
        return seen

    return lax.fori_loop(0, (count + GROUP - 1) // GROUP, group, 0)


def clear_blocks(total, count):
    def clear(p, _):
        total[p] = jnp.zeros((K, TILE), jnp.float32)
        return 0

    lax.fori_loop(0, count, clear, 0, unroll=8)


def forward_spots(blocks):
    return lambda slot, row, col, spare: (slot, col & (blocks - 1), row + N_NAMED * spare)


def forward_near_kernel(codes, scal, tiles, *refs):
    mine_hbm, (total, held, vec, sems, mine, sem) = refs[0], refs[6:]
    pieces = (mine,) + refs[1:6]
    live, x, core = scal[0], scal[1], scal[2]
    chunks = (live + CHUNK - 1) // CHUNK

    def start(chunk, _):
        tile_copy(tiles, held, sems, chunk).start()
        return 0

    def wait(chunk, _):
        tile_copy(tiles, held, sems, chunk).wait()
        return 0

    def ready(seen, need):
        lax.fori_loop(seen, need, wait, 0)
        return jnp.maximum(seen, need)

    fetch = pltpu.make_async_copy(mine_hbm, mine, sem)
    fetch.start()
    lax.fori_loop(0, chunks, start, 0)
    clear_blocks(total, N_NAMED)

    def load(i, d, other):
        first = (((x + d) % N_X) * 2 + (core + other) % 2) * SHARE
        for b in range(SHARE):
            vec[first + b] = pieces[i + 3 * other][:, b * TILE:(b + 1) * TILE]

    for i, d in enumerate(NEAR):
        for other in range(2):
            if i + other:
                load(i, d, other)
    fetch.wait()
    load(0, 0, 0)
    seen = sweep(scal[3], codes, held, vec, total, forward_spots(2 * N_X * SHARE), 1, ready)
    lax.fori_loop(seen, chunks, wait, 0)


def forward_far_kernel(codes, scal, tiles, ids, here, there, begun, send, total, vec):
    core = scal[2]
    for other, piece in enumerate((here, there)):
        first = ((core + other) % 2) * SHARE
        for b in range(SHARE):
            vec[first + b] = piece[:, b * TILE:(b + 1) * TILE]
    sweep(scal[4], codes, tiles, vec, total, forward_spots(2 * SHARE), 1)

    def pack(c, _):
        for q in range(CAP):
            send[c, q * K:(q + 1) * K] = total[c * CAP + q].astype(jnp.bfloat16)
        send[c, RUN_ROWS:] = ids[c]
        return 0

    lax.fori_loop(0, N_COL, pack, 0, unroll=4)


def reduce_kernel(recv, blocks, send, total, wide_ids, ids, sem):
    for c in range(N_COL):
        wide_ids[c:c + 1] = recv[c, RUN_ROWS:][0:1].astype(jnp.float32).astype(jnp.int32)
    copy = pltpu.make_async_copy(wide_ids, ids, sem)
    copy.start()
    for b in range(SHARE):
        total[b] = jnp.zeros((K, TILE), jnp.float32)
    copy.wait()

    def add(c, _):
        spots = [ids[c, q] for q in range(CAP)]
        sums = [total[p] + recv[c, q * K:(q + 1) * K].astype(jnp.float32) for q, p in enumerate(spots)]
        for p, value in zip(spots, sums):
            total[p] = value
        return 0

    lax.fori_loop(0, N_COL, add, 0, unroll=4)
    for b in range(SHARE):
        blocks[b] = total[b].astype(jnp.bfloat16)

    def spread(c, _):
        for q in range(CAP):
            send[c, q * K:(q + 1) * K] = blocks[ids[c, q]]
        return 0

    lax.fori_loop(0, N_COL, spread, 0, unroll=8)


def backward_spots(blocks):
    return lambda slot, row, col, spare: (slot, row, (col & (blocks - 1)) + blocks * spare)


def backward_near_kernel(codes, scal, tiles, recv, keep, give, give_own, total):
    x, core = scal[1], scal[2]
    for d in NEAR:
        clear_blocks(total.at[pl.ds(((x + d) % N_X) * 2 * SHARE, 2 * SHARE)], 2 * SHARE)
    sweep(scal[3], codes, tiles, recv, total, backward_spots(2 * N_X * SHARE), 0)

    def split(b, _):
        for i, d in enumerate(NEAR):
            first = ((x + d) % N_X) * 2 * SHARE + b
            keep[i, b] = total[first + core * SHARE]
            swap = total[first + (1 - core) * SHARE].astype(give.dtype)
            if i:
                give[i - 1, b] = swap
            else:
                give_own[b] = swap
        return 0

    lax.fori_loop(0, SHARE, split, 0, unroll=4)


def backward_far_kernel(codes, scal, tiles, recv, keep, *rest):
    gives, total = rest[:-1], rest[-1]
    core = scal[2]
    clear_blocks(total, 2 * SHARE)
    sweep(scal[4], codes, tiles, recv, total, backward_spots(2 * SHARE), 0)
    part = SHARE // len(gives)

    def split(b, _):
        for i, give in enumerate(gives):
            keep[i * part + b] = total[core * SHARE + i * part + b]
            give[b] = total[(1 - core) * SHARE + i * part + b].astype(give.dtype)
        return 0

    lax.fori_loop(0, part, split, 0, unroll=2)


def side_pair_kernel(keep, got, one, three):
    def step(b, _):
        for i, out in enumerate((one, three)):
            out[b] = (keep[i + 1, b] + got[i, b].astype(jnp.float32)).astype(out.dtype)
        return 0

    lax.fori_loop(0, SHARE, step, 0, unroll=4)


def far_pair_kernel(keep, *rest):
    gots, out = rest[:-1], rest[-1]
    part = SHARE // len(gots)

    def step(b, _):
        for i, got in enumerate(gots):
            out[i * part + b] = (keep[i * part + b] + got[b].astype(jnp.float32)).astype(out.dtype)
        return 0

    lax.fori_loop(0, part, step, 0, unroll=2)


def near_sum_kernel(keep, got, one, three, out):
    def step(b, _):
        out[b] = (
            keep[0, b]
            + got[b].astype(jnp.float32)
            + one[b].astype(jnp.float32)
            + three[b].astype(jnp.float32)
        )
        return 0

    lax.fori_loop(0, SHARE, step, 0, unroll=4)


def final_kernel(begun, two, out):
    for b in range(SHARE):
        total = begun[b] + two[b].astype(jnp.float32)
        out[:, b * TILE:(b + 1) * TILE] = total.astype(jnp.bfloat16)


def call(kernel, outs, scalars, arrays, scratch=(), limit=8, hbm=(), aliases=None, cost=None):
    spec_vmem = pl.BlockSpec(memory_space=pltpu.VMEM)
    spec_smem = pl.BlockSpec(memory_space=pltpu.SMEM)
    spec_hbm = pl.BlockSpec(memory_space=pltpu.HBM)
    specs = [spec_smem] * len(scalars)
    specs += [spec_hbm if i in hbm else spec_vmem for i in range(len(arrays))]
    single = not isinstance(outs, (list, tuple))
    return pl.pallas_call(
        kernel,
        out_shape=outs,
        in_specs=specs,
        out_specs=spec_vmem if single else [spec_vmem] * len(outs),
        scratch_shapes=list(scratch),
        input_output_aliases=aliases or {},
        cost_estimate=cost,
        compiler_params=pltpu.CompilerParams(vmem_limit_bytes=limit << 20),
    )(*scalars, *arrays)


def slot_lists(rowc, cols, live, x):
    slot = jnp.arange(rowc.shape[0], dtype=jnp.int32)
    code = slot | (rowc << 9) | (cols << 17)
    far = (((cols >> 6) - x) & (N_X - 1)) == 2
    member = jnp.stack([(slot < live) & ~far, (slot < live) & far])
    earlier = slot[:, None] < slot[None, :]
    place = jnp.sum(jnp.where(member[:, :, None] & earlier[None], 1, 0), axis=1)
    match = member[:, :, None] & (place[:, :, None] == slot[None, None, :])
    packed = jnp.sum(jnp.where(match, code[None, :, None], 0), axis=1)
    counts = jnp.sum(member.astype(jnp.int32), axis=1)
    return jnp.where(slot[None, :] < counts[:, None], packed, 1 << 25), counts


def named_rows(rows):
    hits = rows[:, None] == jnp.arange(N_COL * SHARE, dtype=jnp.int32)[None, :]
    present = jnp.any(hits, axis=0).astype(jnp.int32).reshape(N_COL, SHARE)
    place = jnp.arange(SHARE, dtype=jnp.int32)
    rank = jnp.sum(jnp.where(place[:, None] < place[None, :], present[:, :, None], 0), axis=1)
    match = (rank[:, None, :] == jnp.arange(CAP, dtype=jnp.int32)[None, :, None]) & (present[:, None, :] > 0)
    ids = jnp.sum(jnp.where(match, place[None, None, :], 0), axis=2)
    position = (rank + CAP * jnp.arange(N_COL, dtype=jnp.int32)[:, None]).reshape(-1)
    rowc = jnp.sum(jnp.where(hits, position[None, :], 0), axis=1)
    return ids, rowc


def per_device(tiles, tile_row, tile_col, tile_count, vectors):
    bf16, f32 = jnp.bfloat16, jnp.float32
    shape = jax.ShapeDtypeStruct
    local = tiles[0, 0]
    rows, cols, live = tile_row[0, 0], tile_col[0, 0], tile_count[0, 0]
    row_at = lax.axis_index("row")
    x, core = row_at // 2, row_at % 2

    def along_x(value, d):
        return lax.ppermute(value, "row", [(i, (i + 2 * d) % 8) for i in range(8)])

    def swap_core(value):
        return lax.ppermute(value, "row", [(i, i ^ 1) for i in range(8)])

    mine = vectors.reshape(K, SHARE * TILE)
    near = [mine, along_x(mine, -1), along_x(mine, 1)]

    ids, rowc = named_rows(rows)
    codes, counts = slot_lists(rowc, cols, live, x)
    scal = jnp.stack([live, x, core, counts[0], counts[1]]).astype(jnp.int32)
    near_codes, far_codes = codes[0], codes[1]
    lanes = jnp.pad(ids, ((0, 0), (0, TILE - CAP))).astype(bf16)
    id_rows = jnp.broadcast_to(lanes[:, None, :], (N_COL, 8, TILE))
    there = swap_core(mine)
    near, there, near_codes, far_codes, id_rows, scal = lax.optimization_barrier(
        (near, there, near_codes, far_codes, id_rows, scal)
    )

    swapped = [there] + [swap_core(v) for v in near[1:]]
    far = along_x(near[1], -1)
    begun, held = call(
        forward_near_kernel,
        [shape((N_NAMED + 1, K, TILE), f32), shape(local.shape, bf16)],
        [near_codes, scal],
        [in_hbm(local), in_hbm(mine)] + near[1:] + swapped,
        [
            pltpu.VMEM((2 * N_X * SHARE, K, TILE), bf16),
            pltpu.SemaphoreType.DMA((local.shape[0] // CHUNK,)),
            pltpu.VMEM((K, SHARE * TILE), bf16),
            pltpu.SemaphoreType.DMA,
        ],
        hbm=(0, 1),
    )
    far, far_there, begun = lax.optimization_barrier((far, along_x(swapped[2], 1), begun))
    send, _ = call(
        forward_far_kernel,
        [shape((N_COL, PAY_ROWS, TILE), bf16), shape((N_NAMED + 1, K, TILE), f32)],
        [far_codes, scal],
        [held, id_rows, far, far_there, begun],
        [pltpu.VMEM((2 * SHARE, K, TILE), bf16)],
        aliases={6: 1},
    )
    recv = lax.all_to_all(send, "col", 0, 0, tiled=True)
    blocks, spread = call(
        reduce_kernel,
        [shape((SHARE, K, TILE), bf16), shape((N_COL, RUN_ROWS, TILE), bf16)],
        [],
        [recv],
        [
            pltpu.VMEM((SHARE, K, TILE), f32),
            pltpu.VMEM((N_COL, TILE), jnp.int32),
            pltpu.SMEM((N_COL, TILE), jnp.int32),
            pltpu.SemaphoreType.DMA,
        ],
    )
    image = call(image_kernel, shape((K, SHARE * TILE), bf16), [], [blocks])
    named = lax.all_to_all(spread, "col", 0, 0, tiled=True).reshape(N_NAMED, K, TILE)

    block = (SHARE, K, TILE)
    wide, narrow = shape(block, f32), shape(block, bf16)
    near_keep, give, give_own = call(
        backward_near_kernel,
        [shape((3,) + block, f32), shape((2,) + block, bf16), narrow],
        [near_codes, scal],
        [held, named],
        [pltpu.VMEM((2 * N_X * SHARE + 1, K, TILE), f32)],
    )
    one, three = call(side_pair_kernel, [narrow, narrow], [], [near_keep, swap_core(give)])
    one, three, named = lax.optimization_barrier((one, three, named))
    one, three = along_x(one, 1), along_x(three, -1)
    keep, *gives = call(
        backward_far_kernel,
        [wide] + [shape((SHARE // PARTS, K, TILE), bf16)] * PARTS,
        [far_codes, scal],
        [held, named],
        [pltpu.VMEM((2 * SHARE + 1, K, TILE), f32)],
        cost=LONG,
    )
    away = call(far_pair_kernel, narrow, [], [keep] + [swap_core(v) for v in gives])
    two = along_x(away, 2)
    begun = call(near_sum_kernel, wide, [], [near_keep, swap_core(give_own), one, three], cost=LONG)
    back = call(final_kernel, shape((K, SHARE * TILE), bf16), [], [begun, two])
    return image, back.reshape(vectors.shape)


def solution(mesh):
    return jax.shard_map(
        per_device,
        mesh=mesh,
        in_specs=(
            P("row", "col", None, None, None),
            P("row", "col", None),
            P("row", "col", None),
            P("row", "col"),
            P(None, "row", "col", None),
        ),
        out_specs=(P(None, ("row", "col")), P(None, "row", "col", None)),
        check_vma=False,
    )
```
